32 devices in a mesh: pair: 8 (over z, x), col: 4 (over y, core).
Axes of the slice: x: 2, y: 2, z: 4, core: 2. Of those that a mesh axis runs over, the one named last changes fastest.
Arguments:
- point_values: bfloat16 [32768, 1024], P('pair', 'col'), may hold values from -2 to 2, as said below
- grid_values: bfloat16 [32768, 512], P('pair'), may hold values from -6 to 6
Outputs:
- fitted: float32 [512, 1024], P(('pair', 'col'))
The draws below stay inside these ranges and needn't reach their ends.
Inputs may be any that keep to these rules, and one draw needn't show every extreme that they name: `point_values`: real pair-product values.
All inputs are finite; a program needn't handle non-finite values.
Results may differ from the reference program's by a relative error of at most 0.0003.
Values may be sent and summed in bfloat16 or wider, within the bound.
A program may use at most 128 MiB of HBM per device.

```python
import math
import jax
import jax.numpy as jnp

NPTS = 1024
PAIRS = 32768
GRID = 512


def draw_point_values(key, part):
    key_noise = jax.random.fold_in(key, 11)
    key_partner = jax.random.fold_in(key, 23)
    key_rows = jax.random.fold_in(key, 37)
    partner = jax.random.permutation(key_partner, NPTS)
    noise_draw = jnp.clip(jax.random.normal(key_noise, (PAIRS, NPTS), jnp.float32), -6.0, 6.0)
    scales = jnp.exp(jax.random.uniform(key_rows, (PAIRS, 1), jnp.float32, 0.0, math.log(4.0)))
    combined = (noise_draw + 0.7 * jnp.take(noise_draw, partner, axis=1)) * scales
    return (combined * (0.35 / math.sqrt(PAIRS))).astype(jnp.bfloat16)


def raised(drawn, stream_key, source, target, parts, factor):
    owner, partner = [(jnp.arange(drawn.shape[axis_at]) // (drawn.shape[axis_at] // parts)).reshape([-1 if axis == axis_at else 1 for axis in range(drawn.ndim)]) for axis_at in (source, target)]
    chosen = jax.random.permutation(stream_key, parts)[partner]
    strong = (owner == chosen) | (owner == (partner + parts // 2) % parts)
    return jnp.where(strong, factor * drawn, drawn)


def levels(key, shape, shards, least, largest):
    loudness, own = 1.0, jax.random.fold_in(key, 6)
    for position, parts in shards:
        draws = jnp.exp(jax.random.uniform(jax.random.fold_in(own, position), (parts,), jnp.float32, least / len(shards), largest / len(shards)))
        loudness = loudness * jnp.repeat(draws, shape[position] // parts).reshape([-1 if axis == position else 1 for axis in range(len(shape))])
    return loudness


def heavy_noise(own_key, extent, spread, reach, cuts, heavy, held_as=jnp.bfloat16):
    entries = spread * jax.random.normal(own_key, extent, jnp.float32)
    if cuts:
        entries = entries * levels(own_key, extent, cuts, -0.22, 0.18)
    return jnp.clip(raised(entries, jax.random.fold_in(own_key, 3), *heavy), -reach, reach).astype(held_as)


def setup_inputs(seed: int = 0) -> dict:
    splits = jax.random.split(jax.random.key(seed), 3)
    return {
        "point_values": draw_point_values(jax.random.fold_in(splits[2], 71), 0),
        "grid_values": heavy_noise(splits[1], (PAIRS, GRID), 1.0, 6.0, ((0, 8),), (0, 1, 8, 2.0)),
    }


def reference(point_values, grid_values):
    gram = jnp.dot(point_values.T.astype(jnp.float32), point_values.astype(jnp.float32), preferred_element_type=jnp.float32)
    factor = jnp.linalg.cholesky(gram)
    project = jnp.dot(grid_values.T.astype(jnp.float32), point_values.astype(jnp.float32), preferred_element_type=jnp.float32)
    solved = jax.scipy.linalg.cho_solve((factor, True), project.T)
    return solved.T
```

```python
import functools

import jax
import jax.numpy as jnp
from jax import lax
from jax.experimental import pallas as pl
from jax.experimental.pallas import tpu as pltpu
from jax.sharding import PartitionSpec as P

NB = 128
TILE = 8
PANEL = 16


def cross(left, right):
    return lax.dot_general(
        left, right, (((0,), (0,)), ((), ())), preferred_element_type=jnp.float32
    )


def dot(left, right, over=0):
    return lax.dot_general(
        left, right, (((1,), (over,)), ((), ())),
        precision=lax.Precision.HIGHEST, preferred_element_type=jnp.float32,
    )


def invert(tiles):
    count, each = len(tiles), PANEL // TILE
    shape = tiles[0].shape
    lane = lax.broadcasted_iota(jnp.int32, shape, 1)
    sub = lax.broadcasted_iota(jnp.int32, shape, 0)

    def column(t, j):
        return jnp.broadcast_to(t[:, j : j + 1], shape)

    def row(t, s):
        return jnp.broadcast_to(t[s : s + 1, :], shape)

    tiles = list(tiles)
    for base in range(0, count, each):
        start = base * TILE
        group = range(base, base + each)
        cols = [[column(tiles[i], start + k) for i in group] for k in range(PANEL)]
        inside = (lane >= start) & (lane < start + PANEL)
        held = [
            jnp.where(inside, jnp.where(lane - i * TILE == sub, 1.0, 0.0), tiles[i])
            for i in group
        ]
        for k in range(PANEL):
            at, s = divmod(k, TILE)
            on_row = sub == s
            inv = 1.0 / row(cols[k][at], s)
            c = list(cols[k])
            c[at] = jnp.where(on_row, -1.0, c[at])

            def sweep(old):
                r = row(old[at], s) * inv
                old = list(old)
                old[at] = jnp.where(on_row, 0.0, old[at])
                return [old[a] - c[a] * r for a in range(each)]

            for m in range(k + 1, PANEL):
                cols[m] = sweep(cols[m])
            held = sweep(held)
        near = range(base + each, min(base + 2 * each, count))
        far = [i for i in range(count) if i not in group and i not in near]
        for i in near:
            part = [jnp.where(inside, 0.0, tiles[i]), jnp.zeros(shape, jnp.float32)]
            for k in range(PANEL):
                at, s = divmod(k, TILE)
                part[k % 2] -= column(tiles[i], start + k) * row(held[at], s)
            tiles[i] = part[0] + part[1]
        if far:
            left = jnp.concatenate([jnp.where(inside, tiles[i], 0.0) for i in far], axis=0)
            zero = jnp.zeros(shape, jnp.float32)
            right = jnp.concatenate(
                [held[i - base] if i in group else zero for i in range(count)], axis=0
            )
            product = dot(left, right)
            for q, i in enumerate(far):
                tiles[i] = jnp.where(inside, 0.0, tiles[i]) - product[q * TILE : (q + 1) * TILE]
        for i in group:
            tiles[i] = held[i - base]
    return tiles


def eliminate(work, inverse, n, rows, out_ref):
    def step(k, carry):
        for kk in range(n // NB):
            @pl.when(k == kk)
            def _():
                inverse[...] = work[kk * NB : (kk + 1) * NB, kk * NB : (kk + 1) * NB]

        tiles = invert([inverse[i : i + TILE, :] for i in range(0, NB, TILE)])
        for i, t in enumerate(tiles):
            inverse[i * TILE : (i + 1) * TILE, :] = t

        for kk in range(n // NB):
            lo = kk // 2 * 2 * NB
            mid, hi = lo + NB, lo + 2 * NB

            @pl.when(k == kk)
            def _():
                if kk % 2 == 0:
                    below = work[mid:hi, lo:mid]
                    scaled = dot(below, inverse[...])
                    work[mid:hi, lo:mid] = scaled
                    work[lo:mid, lo:mid] = inverse[...]
                    work[mid:hi, mid:hi] -= dot(scaled, below, 1)
                    return
                scaled = work[mid:hi, lo:mid]
                corner = dot(inverse[...], scaled)
                work[lo:mid, lo:mid] += dot(scaled.T, corner)
                work[lo:mid, mid:hi] = -corner.T
                work[mid:hi, lo:mid] = -corner
                work[mid:hi, mid:hi] = inverse[...]
                below = work[hi : n + rows, lo:hi]
                ratio = dot(below, work[lo:hi, lo:hi])
                for at in range(hi, n, 2 * NB):
                    work[at : n + rows, at : at + 2 * NB] -= dot(
                        ratio[at - hi :], below[at - hi : at - hi + 2 * NB], 1
                    )
                work[hi : n + rows, lo:hi] = ratio
        return carry

    lax.fori_loop(0, n // NB, step, 0)
    for lo in range(n - 2 * NB, -1, -2 * NB):
        hi = lo + 2 * NB
        x = work[n : n + rows, lo:hi]
        if hi < n:
            x = x - dot(out_ref[:, hi:n], work[hi:n, lo:hi])
        out_ref[:, lo:hi] = x


def solve_kernel(cols, folded, gram_ref, rhs_ref, out_ref, work, inverse):
    n = work.shape[1]
    rows = rhs_ref.shape[0]
    blocks = n // NB
    width = n // cols
    height = gram_ref.shape[1]
    if folded:
        half = width // 2
        quarter = half // 2

        def put(row, col, block):
            h, w = block.shape
            work[row : row + h, col : col + w] = block

        held = []
        for c in range(cols):
            held.append(jnp.concatenate(
                [gram_ref[p * cols + c] for p in range(gram_ref.shape[0] // cols)], axis=0
            ))
        cross_at = half + quarter + half
        for c in range(cols):
            at = c * width
            low = held[c][:half]
            corner = held[c][half : half + quarter]
            put(at + half, at, low)
            put(at, at + half, low[:, :half].T)
            put(at, at, corner[:, :half])
            put(at + quarter, at, corner[:, half:])
        for c in (0, 2):
            both = jnp.concatenate(
                [held[c + core][half + quarter : cross_at] for core in range(2)], axis=0
            )
            put(c * width, (c + 1) * width, both)
            put((c + 1) * width, c * width, both.T)
        for part in (2, 3):
            first = cross_at + (part - 2) * width
            for c in range(2):
                row, col = c ^ 2, c ^ (part - 2)
                total = held[c][first : first + width] + held[c ^ part][first : first + width].T
                put(row * width, col * width, total)
                put(col * width, row * width, total.T)
    else:
        for i in range(gram_ref.shape[0]):
            p, c = divmod(i, cols)
            work[p * height : (p + 1) * height, c * width : (c + 1) * width] = gram_ref[i]
    work[n : n + rows, :] = rhs_ref[...]

    eliminate(work, inverse, n, rows, out_ref)


def solve(gram_parts, rhs, cols, folded):
    rows, n = rhs.shape
    vmem = pl.BlockSpec(memory_space=pltpu.VMEM)
    return pl.pallas_call(
        functools.partial(solve_kernel, cols, folded),
        out_shape=jax.ShapeDtypeStruct((rows, n), jnp.float32),
        in_specs=[vmem, vmem],
        out_specs=vmem,
        scratch_shapes=[
            pltpu.VMEM((n + rows, n), jnp.float32),
            pltpu.VMEM((NB, NB), jnp.float32),
        ],
        compiler_params=pltpu.CompilerParams(vmem_limit_bytes=48 << 20),
    )(gram_parts, rhs)


def fold(own):
    c = lax.axis_index("col")
    half = own.shape[0] // 2
    y = c // 2
    other = lax.dynamic_slice_in_dim(own, (1 - y) * half, half, 0)
    received = lax.ppermute(other, "col", [(i, i ^ 2) for i in range(4)])
    sibling = lax.ppermute(own, "col", [(i, i ^ 1) for i in range(4)])
    own_half = lax.dynamic_slice_in_dim(own, y * half, half, 0)
    sibling_half = lax.dynamic_slice_in_dim(sibling, y * half, half, 0)
    square = cross(own, own)
    width = square.shape[0]
    mid = width // 2
    corner = square[:mid, :mid]
    corner = jnp.concatenate([corner[: mid // 2], corner[mid // 2 :]], axis=1)
    beside = cross(sibling, own)
    beside = jnp.where(c % 2 == 0, beside.T[:mid], beside[mid:])
    return jnp.concatenate(
        [square[mid:], corner, beside, cross(received, own_half), cross(received, sibling_half)],
        axis=0,
    )


def solution(mesh):
    cols, pairs = mesh.shape["col"], mesh.shape["pair"]
    folded = cols == 4 and pairs == 8

    def body(point_values, grid_values):
        project = cross(grid_values, point_values)
        if folded:
            gram = fold(point_values)
        else:
            gathered = lax.all_gather(point_values, "col", axis=1, tiled=True)
            gram = cross(gathered, point_values)
        width = gram.shape[1]
        both = jnp.concatenate(
            [gram.reshape(pairs, -1, width), project.reshape(pairs, -1, width)], axis=1
        )
        exchanged = lax.all_to_all(both, "pair", split_axis=0, concat_axis=0, tiled=True)
        own = jnp.sum(exchanged, axis=0)
        height = gram.shape[0] // pairs
        gram_parts = lax.all_gather(own[:height], ("pair", "col"), axis=0, tiled=False)
        regrouped = lax.all_to_all(own[height:], "col", split_axis=0, concat_axis=1, tiled=True)
        return solve(gram_parts, regrouped, cols, folded)

    in_specs = (P("pair", "col"), P("pair", None))
    out_specs = P(("pair", "col"), None)
    return jax.shard_map(body, mesh=mesh, in_specs=in_specs, out_specs=out_specs, check_vma=False)
```

```python
import functools

import jax
import jax.numpy as jnp
from jax import lax
from jax.experimental import pallas as pl
from jax.experimental.pallas import tpu as pltpu
from jax.sharding import PartitionSpec as P

NB = 128
TILE = 8
PANEL = 16
CHUNK = 1024
MESH = pl.DeviceIdType.MESH


def cross(left, right):
    return lax.dot_general(
        left, right, (((0,), (0,)), ((), ())), preferred_element_type=jnp.float32
    )


def dot(left, right, over=0):
    return lax.dot_general(
        left, right, (((1,), (over,)), ((), ())),
        precision=lax.Precision.HIGHEST, preferred_element_type=jnp.float32,
    )


def invert(tiles):
    count, each = len(tiles), PANEL // TILE
    shape = tiles[0].shape
    lane = lax.broadcasted_iota(jnp.int32, shape, 1)
    sub = lax.broadcasted_iota(jnp.int32, shape, 0)

    def column(t, j):
        return jnp.broadcast_to(t[:, j : j + 1], shape)

    def row(t, s):
        return jnp.broadcast_to(t[s : s + 1, :], shape)

    tiles = list(tiles)
    for base in range(0, count, each):
        start = base * TILE
        group = range(base, base + each)
        cols = [[column(tiles[i], start + k) for i in group] for k in range(PANEL)]
        inside = (lane >= start) & (lane < start + PANEL)
        held = [
            jnp.where(inside, jnp.where(lane - i * TILE == sub, 1.0, 0.0), tiles[i])
            for i in group
        ]
        for k in range(PANEL):
            at, s = divmod(k, TILE)
            on_row = sub == s
            inv = 1.0 / row(cols[k][at], s)
            c = list(cols[k])
            c[at] = jnp.where(on_row, -1.0, c[at])

            def sweep(old):
                r = row(old[at], s) * inv
                old = list(old)
                old[at] = jnp.where(on_row, 0.0, old[at])
                return [old[a] - c[a] * r for a in range(each)]

            for m in range(k + 1, PANEL):
                cols[m] = sweep(cols[m])
            held = sweep(held)
        near = range(base + each, min(base + 2 * each, count))
        far = [i for i in range(count) if i not in group and i not in near]
        for i in near:
            part = [jnp.where(inside, 0.0, tiles[i]), jnp.zeros(shape, jnp.float32)]
            for k in range(PANEL):
                at, s = divmod(k, TILE)
                part[k % 2] -= column(tiles[i], start + k) * row(held[at], s)
            tiles[i] = part[0] + part[1]
        if far:
            left = jnp.concatenate([jnp.where(inside, tiles[i], 0.0) for i in far], axis=0)
            zero = jnp.zeros(shape, jnp.float32)
            right = jnp.concatenate(
                [held[i - base] if i in group else zero for i in range(count)], axis=0
            )
            product = dot(left, right)
            for q, i in enumerate(far):
                tiles[i] = jnp.where(inside, 0.0, tiles[i]) - product[q * TILE : (q + 1) * TILE]
        for i in group:
            tiles[i] = held[i - base]
    return tiles


def eliminate(work, inverse, n, rows, first=0, hooks=()):
    def step(k, carry):
        for at, hook in hooks:
            pl.when(k == at)(hook)
        for kk in range(n // NB):
            @pl.when(k == kk)
            def _():
                inverse[...] = work[kk * NB : (kk + 1) * NB, kk * NB : (kk + 1) * NB]

        tiles = invert([inverse[i : i + TILE, :] for i in range(0, NB, TILE)])
        for i, t in enumerate(tiles):
            inverse[i * TILE : (i + 1) * TILE, :] = t

        for kk in range(n // NB):
            lo = kk // 2 * 2 * NB
            mid, hi = lo + NB, lo + 2 * NB
            end, limit = (first, first) if lo < first else (n, n + rows)

            @pl.when(k == kk)
            def _():
                if kk % 2 == 0:
                    below = work[mid:hi, lo:mid]
                    scaled = dot(below, inverse[...])
                    work[mid:hi, lo:mid] = scaled
                    work[lo:mid, lo:mid] = inverse[...]
                    work[mid:hi, mid:hi] -= dot(scaled, below, 1)
                    return
                scaled = work[mid:hi, lo:mid]
                corner = dot(inverse[...], scaled)
                work[lo:mid, lo:mid] += dot(scaled.T, corner)
                work[lo:mid, mid:hi] = -corner.T
                work[mid:hi, lo:mid] = -corner
                work[mid:hi, mid:hi] = inverse[...]
                if hi == limit:
                    return
                below = work[hi:limit, lo:hi]
                ratio = dot(below, work[lo:hi, lo:hi])
                for at in range(hi, end, 2 * NB):
                    work[at:limit, at : at + 2 * NB] -= dot(
                        ratio[at - hi :], below[at - hi : at - hi + 2 * NB], 1
                    )
                work[hi:limit, lo:hi] = ratio
        return carry

    lax.fori_loop(0, n // NB, step, 0)


def substitute(work, n, rows, out_ref):
    for lo in range(n - 2 * NB, -1, -2 * NB):
        hi = lo + 2 * NB
        x = work[n : n + rows, lo:hi]
        if hi < n:
            x = x - dot(out_ref[:, hi:n], work[hi:n, lo:hi])
        out_ref[:, lo:hi] = x


def solve_kernel(cols, gram_ref, rhs_ref, out_ref, work, inverse):
    n = work.shape[1]
    rows = rhs_ref.shape[0]
    width = n // cols
    height = gram_ref.shape[1]
    for i in range(gram_ref.shape[0]):
        p, c = divmod(i, cols)
        work[p * height : (p + 1) * height, c * width : (c + 1) * width] = gram_ref[i]
    work[n : n + rows, :] = rhs_ref[...]
    eliminate(work, inverse, n, rows)
    substitute(work, n, rows, out_ref)


def solve(gram_parts, rhs, cols):
    rows, n = rhs.shape
    vmem = pl.BlockSpec(memory_space=pltpu.VMEM)
    return pl.pallas_call(
        functools.partial(solve_kernel, cols),
        out_shape=jax.ShapeDtypeStruct((rows, n), jnp.float32),
        in_specs=[vmem, vmem],
        out_specs=vmem,
        scratch_shapes=[
            pltpu.VMEM((n + rows, n), jnp.float32),
            pltpu.VMEM((NB, NB), jnp.float32),
        ],
        compiler_params=pltpu.CompilerParams(vmem_limit_bytes=48 << 20),
    )(gram_parts, rhs)


def flip(index, mask):
    total = 0
    for bit in (4, 2, 1):
        own = index // bit % 2
        total = total + bit * (1 - own if mask & bit else own)
    return total


def accumulate(total, left, right, start, count):
    total[...] = jnp.zeros_like(total)

    def chunk(i, carry):
        at = pl.ds(pl.multiple_of(start + i * CHUNK, CHUNK), CHUNK)
        total[...] += cross(left(at), right(at))
        return carry

    lax.fori_loop(0, count // CHUNK, chunk, 0)


def fused_kernel(
    point_ref, grid_ref, out_ref,
    own, sibling, received, grid, total, square_part, beside_part, project_part, cross_part,
    square_in, beside_in, project_in, cross_in, pair_sum, pair_in, project_sum, rhs_in,
    early, other, late, work, inverse, local_sem, send_sem, recv_sem,
):
    p, c = lax.axis_index("pair"), lax.axis_index("col")
    z, x, y, k = p // 2, p % 2, c // 2, c % 2
    count, width = own.shape
    n = work.shape[1]
    rows = out_ref.shape[0]
    mid, half = width // 2, n // 2

    barrier = pltpu.get_barrier_semaphore()
    friends = [(flip(p, d), c) for d in range(1, 8)] + [(p, flip(c, d)) for d in range(1, 4)]
    for friend in friends:
        pl.semaphore_signal(barrier, inc=1, device_id=friend, device_id_type=MESH)
    pl.semaphore_wait(barrier, len(friends))

    used = []

    def copy(at, src, dst, device):
        return pltpu.make_async_remote_copy(
            src_ref=src, dst_ref=dst, send_sem=send_sem.at[at], recv_sem=recv_sem.at[at],
            device_id=device, device_id_type=MESH,
        )

    def plan(*copies):
        base = len(used)
        used.extend(copies)
        return [functools.partial(copy, base + i, *args) for i, args in enumerate(copies)]

    def start(copies):
        for make in copies:
            make().start()

    def arrive(copies):
        for make in copies:
            make().wait_recv()

    away = pl.ds(pl.multiple_of((1 - y) * (count // 2), count // 2), count // 2)
    far = plan((point_ref.at[away, :], received, (p, flip(c, 2))))
    beside = plan((point_ref, sibling, (p, flip(c, 1))))

    def scatter(part, landed):
        return plan(*[
            (part.at[flip(p, d)], landed.at[d - 1], (flip(p, d), c)) for d in range(1, 8)
        ])

    square_out = scatter(square_part, square_in)
    beside_out = scatter(beside_part, beside_in)
    project_out = scatter(project_part, project_in)
    cross_out = scatter(cross_part, cross_in)

    def over_z(slots):
        return plan(*[(slots, slots, (flip(z, d) * 2 + x, c)) for d in range(1, 4)])

    mine = early.at[k, x, z]
    early_z = over_z(mine)
    early_x = plan((early.at[k, x], early.at[k, x], (flip(p, 1), c)))
    early_core = plan((early.at[k], early.at[k], (p, flip(c, 1))))
    early_y = plan((early.at[k], other.at[k], (p, flip(c, 2))))
    other_core = plan((other.at[k], other.at[k], (p, flip(c, 1))))

    height = project_sum.shape[0] // 4

    def share(index):
        return project_sum.at[pl.ds(pl.multiple_of(index * height, height), height)]

    rhs_out = plan(*[
        (share(flip(c, d)), rhs_in.at[c], (p, flip(c, d))) for d in range(1, 4)
    ])
    depth = pair_in.shape[1]
    give = pl.ds(pl.multiple_of((1 - y) * depth, depth), depth)
    keep = pl.ds(pl.multiple_of(y * depth, depth), depth)
    pair_out = plan(
        (pair_sum.at[0, give], pair_in.at[0], (p, flip(c, 2))),
        (pair_sum.at[1, give], pair_in.at[1], (p, flip(c, 3))),
    )
    late_z = over_z(late.at[k, y, x, z])
    late_plane = plan(
        (late.at[k, y, x], late.at[k, y, x], (flip(p, 1), c)),
        (late.at[k, y, x], late.at[k, y, x], (p, flip(c, 2))),
    )
    first, second = pl.ds(0, 2), pl.ds(2, 2)
    late_on = plan(
        (late.at[k, y, 1 - x, first], late.at[k, y, 1 - x, first], (p, flip(c, 2))),
        (late.at[k, 1 - y, x, second], late.at[k, 1 - y, x, second], (flip(p, 1), c)),
    )
    late_core = plan((late.at[k], late.at[k], (p, flip(c, 1))))

    def load(i, src, dst):
        return pltpu.make_async_copy(src, dst, local_sem.at[i])

    start(far)
    load(0, point_ref, own).start()
    start(beside)
    load(1, grid_ref, grid).start()

    def deal(part, value):
        step = value.shape[0] // 8
        for q in range(8):
            part[q] = value[q * step : (q + 1) * step]

    load(0, point_ref, own).wait()
    accumulate(total, lambda at: own[at, :], lambda at: own[at, :], 0, count)
    square = total[...]
    corner = jnp.concatenate([square[: mid // 2, :mid], square[mid // 2 : mid, :mid]], axis=1)
    deal(square_part, jnp.concatenate([square[mid:], corner], axis=0))
    start(square_out)

    arrive(beside)
    upper = total.at[pl.ds(0, mid)]

    @pl.when(k == 0)
    def _():
        accumulate(upper, lambda at: sibling[at, mid:], lambda at: own[at, :], 0, count)

    @pl.when(k == 1)
    def _():
        accumulate(upper, lambda at: own[at, :mid], lambda at: sibling[at, :], 0, count)

    deal(beside_part, upper[...])
    start(beside_out)

    load(1, grid_ref, grid).wait()
    tall = work.at[pl.ds(0, grid.shape[1]), pl.ds(0, width)]
    accumulate(tall, lambda at: grid[at, :], lambda at: own[at, :], 0, count)
    deal(project_part, tall[...])

    def gathered(part, landed):
        value = part[p]
        for d in range(7):
            value = value + landed[d]
        return value

    cut = square_part.shape[1]
    arrive(square_out)
    mine[:cut] = gathered(square_part, square_in)
    arrive(beside_out)
    mine[cut:] = gathered(beside_part, beside_in)
    start(early_z)
    arrive(early_z)
    start(early_x)
    arrive(early_x)
    start(early_core)
    start(early_y)
    start(project_out)
    arrive(early_core)

    def place(slots, at):
        def block(core, part):
            return jnp.concatenate([slots[core, q % 2, q // 2, part] for q in range(8)], axis=0)

        for core in range(2):
            lo = at + core * width
            held = block(core, slice(0, cut))
            work[lo + mid : lo + width, lo : lo + width] = held[:mid]
            work[lo : lo + mid // 2, lo : lo + mid] = held[mid:, :mid]
            work[lo + mid // 2 : lo + mid, lo : lo + mid] = held[mid:, mid:]
        lo, hi = at, at + width
        work[hi : hi + mid, lo:hi] = block(1, slice(cut, None))
        work[hi + mid : hi + width, lo:hi] = block(0, slice(cut, None))

    place(early, 0)

    def cross_terms():
        arrive(far)
        start_at = y * (count // 2)

        def terms(block, left, right):
            def chunk(i, carry):
                there = pl.ds(pl.multiple_of(i * CHUNK, CHUNK), CHUNK)
                here = pl.ds(pl.multiple_of(start_at + i * CHUNK, CHUNK), CHUNK)
                total[...] += cross(left(here, there), right(here, there))
                return carry

            total[...] = jnp.zeros_like(total)
            lax.fori_loop(0, count // 2 // CHUNK, chunk, 0)
            step = width // 8
            for q in range(8):
                cross_part[q, block] = total[q * step : (q + 1) * step, :]

        for block, ours in ((0, own), (1, sibling)):
            @pl.when(y == 0)
            def _():
                terms(block, lambda h, t: received[t, :], lambda h, t: ours[h, :])

            @pl.when(y == 1)
            def _():
                terms(block, lambda h, t: ours[h, :], lambda h, t: received[t, :])

        start(cross_out)

    def right_sides():
        arrive(early_y)
        start(other_core)
        arrive(project_out)
        project_sum[...] = gathered(project_part, project_in)
        start(rhs_out)
        rhs_in[c] = share(c)[...]

    def join():
        arrive(cross_out)
        pair_sum[...] = gathered(cross_part, cross_in)
        start(pair_out)
        arrive(pair_out)
        for block in range(2):
            late[k, y, x, z, block * depth : (block + 1) * depth] = (
                pair_sum[block, keep] + pair_in[block]
            )
        start(late_z)
        arrive(late_z)
        start(late_plane)
        arrive(late_plane)
        start(late_on)
        arrive(late_on)
        start(late_core)
        arrive(other_core)
        place(other, half)
        arrive(rhs_out)
        for col in range(4):
            @pl.when(y == 0)
            def _():
                work[n : n + rows, col * width : (col + 1) * width] = rhs_in[col]

            @pl.when(y == 1)
            def _():
                work[n : n + rows, (col ^ 2) * width : ((col ^ 2) + 1) * width] = rhs_in[col]

        arrive(late_core)
        for i in range(2):
            for j in range(2):
                pieces = []
                for q in range(8):
                    for side in range(2):
                        core = i if i == j or side == 0 else j
                        block = 0 if i == j else 1
                        pieces.append(late[
                            core, side, q % 2, q // 2, block * depth : (block + 1) * depth
                        ])
                value = jnp.concatenate(pieces, axis=0)

                @pl.when(y == 0)
                def _():
                    work[half + i * width : half + (i + 1) * width, j * width : (j + 1) * width] = value

                @pl.when(y == 1)
                def _():
                    work[half + j * width : half + (j + 1) * width, i * width : (i + 1) * width] = value.T

        limit = n + rows
        low = work[half:limit, :width]
        high = work[half:limit, width:half] - dot(low, work[width:half, :width], 1)
        low_ratio = dot(low, work[:width, :width])
        high_ratio = dot(high, work[width:half, width:half])
        for at in range(half, n, width):
            cut_at = at - half
            work[at:limit, at : at + width] -= dot(
                low_ratio[cut_at:], low[cut_at : cut_at + width], 1
            ) + dot(high_ratio[cut_at:], high[cut_at : cut_at + width], 1)
        work[half:limit, :width] = low_ratio
        work[half:limit, width:half] = high_ratio

    eliminate(work, inverse, n, rows, half, ((2, cross_terms), (3, right_sides), (4, join)))
    solved = work.at[pl.ds(0, rows)]
    substitute(work, n, rows, solved)

    @pl.when(y == 0)
    def _():
        out_ref[...] = solved[...]

    @pl.when(y == 1)
    def _():
        out_ref[:, :half] = solved[:, half:]
        out_ref[:, half:] = solved[:, :half]

    for i, args in enumerate(used):
        copy(i, *args).wait_send()


def fused(point_values, grid_values):
    count, width = point_values.shape
    rows_all = grid_values.shape[1]
    n = 4 * width
    rows = rows_all // 32
    cut, side, deep, slot = width * 3 // 32, width // 16, width // 8, width // 8
    f32, bf16 = jnp.float32, jnp.bfloat16

    def buffer(*shape, dtype=f32):
        return pltpu.VMEM(shape, dtype)

    hbm = pl.BlockSpec(memory_space=pl.ANY)
    return pl.pallas_call(
        fused_kernel,
        out_shape=jax.ShapeDtypeStruct((rows, n), f32),
        in_specs=[hbm, hbm],
        out_specs=pl.BlockSpec(memory_space=pltpu.VMEM),
        scratch_shapes=[
            buffer(count, width, dtype=bf16),
            buffer(count, width, dtype=bf16),
            buffer(count // 2, width, dtype=bf16),
            buffer(count, rows_all, dtype=bf16),
            buffer(width, width),
            buffer(8, cut, width),
            buffer(8, side, width),
            buffer(8, rows_all // 8, width),
            buffer(8, 2, deep, width),
            buffer(7, cut, width),
            buffer(7, side, width),
            buffer(7, rows_all // 8, width),
            buffer(7, 2, deep, width),
            buffer(2, deep, width),
            buffer(2, deep // 2, width),
            buffer(rows_all // 8, width),
            buffer(4, rows, width),
            buffer(2, 2, 4, cut + side, width),
            buffer(2, 2, 4, cut + side, width),
            buffer(2, 2, 2, 4, slot, width),
            buffer(n + rows, n),
            buffer(NB, NB),
            pltpu.SemaphoreType.DMA((2,)),
            pltpu.SemaphoreType.DMA((56,)),
            pltpu.SemaphoreType.DMA((56,)),
        ],
        compiler_params=pltpu.CompilerParams(
            collective_id=0, has_side_effects=True, vmem_limit_bytes=48 << 20
        ),
    )(point_values, grid_values)


def solution(mesh):
    cols, pairs = mesh.shape["col"], mesh.shape["pair"]

    def body(point_values, grid_values):
        if cols == 4 and pairs == 8:
            return fused(point_values, grid_values)
        project = cross(grid_values, point_values)
        gathered = lax.all_gather(point_values, "col", axis=1, tiled=True)
        gram = cross(gathered, point_values)
        width = gram.shape[1]
        both = jnp.concatenate(
            [gram.reshape(pairs, -1, width), project.reshape(pairs, -1, width)], axis=1
        )
        exchanged = lax.all_to_all(both, "pair", split_axis=0, concat_axis=0, tiled=True)
        own = jnp.sum(exchanged, axis=0)
        height = gram.shape[0] // pairs
        gram_parts = lax.all_gather(own[:height], ("pair", "col"), axis=0, tiled=False)
        regrouped = lax.all_to_all(own[height:], "col", split_axis=0, concat_axis=1, tiled=True)
        return solve(gram_parts, regrouped, cols)

    in_specs = (P("pair", "col"), P("pair", None))
    out_specs = P(("pair", "col"), None)
    return jax.shard_map(body, mesh=mesh, in_specs=in_specs, out_specs=out_specs, check_vma=False)
```

```python
import functools

import jax
import jax.numpy as jnp
from jax import lax
from jax.experimental import pallas as pl
from jax.experimental.pallas import tpu as pltpu
from jax.sharding import PartitionSpec as P

NB = 128
TILE = 8
PANEL = 16
CHUNK = 1024
MESH = pl.DeviceIdType.MESH


def cross(left, right):
    return lax.dot_general(
        left, right, (((0,), (0,)), ((), ())), preferred_element_type=jnp.float32
    )


def dot(left, right, over=0):
    return lax.dot_general(
        left, right, (((1,), (over,)), ((), ())),
        precision=lax.Precision.HIGHEST, preferred_element_type=jnp.float32,
    )


def invert(tiles):
    count, each = len(tiles), PANEL // TILE
    shape = tiles[0].shape
    lane = lax.broadcasted_iota(jnp.int32, shape, 1)
    sub = lax.broadcasted_iota(jnp.int32, shape, 0)

    def column(t, j):
        return jnp.broadcast_to(t[:, j : j + 1], shape)

    def row(t, s):
        return jnp.broadcast_to(t[s : s + 1, :], shape)

    tiles = list(tiles)
    for base in range(0, count, each):
        start = base * TILE
        group = range(base, base + each)
        cols = [[column(tiles[i], start + k) for i in group] for k in range(PANEL)]
        inside = (lane >= start) & (lane < start + PANEL)
        held = [
            jnp.where(inside, jnp.where(lane - i * TILE == sub, 1.0, 0.0), tiles[i])
            for i in group
        ]
        for k in range(PANEL):
            at, s = divmod(k, TILE)
            on_row = sub == s
            inv = 1.0 / row(cols[k][at], s)
            c = list(cols[k])
            c[at] = jnp.where(on_row, -1.0, c[at])

            def sweep(old):
                r = row(old[at], s) * inv
                old = list(old)
                old[at] = jnp.where(on_row, 0.0, old[at])
                return [old[a] - c[a] * r for a in range(each)]

            for m in range(k + 1, PANEL):
                cols[m] = sweep(cols[m])
            held = sweep(held)
        near = range(base + each, min(base + 2 * each, count))
        far = [i for i in range(count) if i not in group and i not in near]
        for i in near:
            part = [jnp.where(inside, 0.0, tiles[i]), jnp.zeros(shape, jnp.float32)]
            for k in range(PANEL):
                at, s = divmod(k, TILE)
                part[k % 2] -= column(tiles[i], start + k) * row(held[at], s)
            tiles[i] = part[0] + part[1]
        if far:
            left = jnp.concatenate([jnp.where(inside, tiles[i], 0.0) for i in far], axis=0)
            zero = jnp.zeros(shape, jnp.float32)
            right = jnp.concatenate(
                [held[i - base] if i in group else zero for i in range(count)], axis=0
            )
            product = dot(left, right)
            for q, i in enumerate(far):
                tiles[i] = jnp.where(inside, 0.0, tiles[i]) - product[q * TILE : (q + 1) * TILE]
        for i in group:
            tiles[i] = held[i - base]
    return tiles


def eliminate(work, inverse, n, rows, first=0, hooks=()):
    def step(k, carry):
        for at, hook in hooks:
            pl.when(k == at)(hook)
        for kk in range(n // NB):
            @pl.when(k == kk)
            def _():
                inverse[...] = work[kk * NB : (kk + 1) * NB, kk * NB : (kk + 1) * NB]

        tiles = invert([inverse[i : i + TILE, :] for i in range(0, NB, TILE)])
        for i, t in enumerate(tiles):
            inverse[i * TILE : (i + 1) * TILE, :] = t

        for kk in range(n // NB):
            lo = kk // 2 * 2 * NB
            mid, hi = lo + NB, lo + 2 * NB
            end, limit = (first, first) if lo < first else (n, n + rows)

            @pl.when(k == kk)
            def _():
                if kk % 2 == 0:
                    below = work[mid:hi, lo:mid]
                    scaled = dot(below, inverse[...])
                    work[mid:hi, lo:mid] = scaled
                    work[lo:mid, lo:mid] = inverse[...]
                    work[mid:hi, mid:hi] -= dot(scaled, below, 1)
                    return
                scaled = work[mid:hi, lo:mid]
                corner = dot(inverse[...], scaled)
                work[lo:mid, lo:mid] += dot(scaled.T, corner)
                work[lo:mid, mid:hi] = -corner.T
                work[mid:hi, lo:mid] = -corner
                work[mid:hi, mid:hi] = inverse[...]
                if hi == limit:
                    return
                below = work[hi:limit, lo:hi]
                ratio = dot(below, work[lo:hi, lo:hi])
                for at in range(hi, end, 2 * NB):
                    work[at:limit, at : at + 2 * NB] -= dot(
                        ratio[at - hi :], below[at - hi : at - hi + 2 * NB], 1
                    )
                work[hi:limit, lo:hi] = ratio
        return carry

    lax.fori_loop(0, n // NB, step, 0)


def substitute(work, n, rows, out_ref):
    for lo in range(n - 2 * NB, -1, -2 * NB):
        hi = lo + 2 * NB
        x = work[n : n + rows, lo:hi]
        if hi < n:
            x = x - dot(out_ref[:, hi:n], work[hi:n, lo:hi])
        out_ref[:, lo:hi] = x


def solve_kernel(cols, gram_ref, rhs_ref, out_ref, work, inverse):
    n = work.shape[1]
    rows = rhs_ref.shape[0]
    width = n // cols
    height = gram_ref.shape[1]
    for i in range(gram_ref.shape[0]):
        p, c = divmod(i, cols)
        work[p * height : (p + 1) * height, c * width : (c + 1) * width] = gram_ref[i]
    work[n : n + rows, :] = rhs_ref[...]
    eliminate(work, inverse, n, rows)
    substitute(work, n, rows, out_ref)


def solve(gram_parts, rhs, cols):
    rows, n = rhs.shape
    vmem = pl.BlockSpec(memory_space=pltpu.VMEM)
    return pl.pallas_call(
        functools.partial(solve_kernel, cols),
        out_shape=jax.ShapeDtypeStruct((rows, n), jnp.float32),
        in_specs=[vmem, vmem],
        out_specs=vmem,
        scratch_shapes=[
            pltpu.VMEM((n + rows, n), jnp.float32),
            pltpu.VMEM((NB, NB), jnp.float32),
        ],
        compiler_params=pltpu.CompilerParams(vmem_limit_bytes=48 << 20),
    )(gram_parts, rhs)


def flip(index, mask):
    total = 0
    for bit in (4, 2, 1):
        own = index // bit % 2
        total = total + bit * (1 - own if mask & bit else own)
    return total


def accumulate(total, left, right, start, count):
    total[...] = jnp.zeros_like(total)

    def chunk(i, carry):
        at = pl.ds(pl.multiple_of(start + i * CHUNK, CHUNK), CHUNK)
        total[...] += cross(left(at), right(at))
        return carry

    lax.fori_loop(0, count // CHUNK, chunk, 0)


def fused_kernel(
    point_ref, grid_ref, out_ref,
    own, sibling, received, grid, total, square_part, beside_part, project_part, cross_part,
    square_in, beside_in, project_in_x, project_in_z, cross_in, pair_sum, pair_in,
    project_sum, rhs_in,
    early, other, late, work, inverse, local_sem, send_sem, recv_sem,
):
    p, c = lax.axis_index("pair"), lax.axis_index("col")
    z, x, y, k = p // 2, p % 2, c // 2, c % 2
    count, width = own.shape
    n = work.shape[1]
    rows = out_ref.shape[0]
    mid, half = width // 2, n // 2

    barrier = pltpu.get_barrier_semaphore()
    friends = [(flip(p, d), c) for d in range(1, 8)] + [(p, flip(c, d)) for d in range(1, 4)]
    for friend in friends:
        pl.semaphore_signal(barrier, inc=1, device_id=friend, device_id_type=MESH)
    pl.semaphore_wait(barrier, len(friends))

    used = []

    def copy(at, src, dst, device):
        return pltpu.make_async_remote_copy(
            src_ref=src, dst_ref=dst, send_sem=send_sem.at[at], recv_sem=recv_sem.at[at],
            device_id=device, device_id_type=MESH,
        )

    def plan(*copies):
        base = len(used)
        used.extend(copies)
        return [functools.partial(copy, base + i, *args) for i, args in enumerate(copies)]

    def start(copies):
        for make in copies:
            make().start()

    def arrive(copies):
        for make in copies:
            make().wait_recv()

    away = pl.ds(pl.multiple_of((1 - y) * (count // 2), count // 2), count // 2)
    far = [
        plan((point_ref.at[away, pl.ds(h * mid, mid)], received.at[h], (p, flip(c, 2))))
        for h in range(2)
    ]
    beside = plan((point_ref, sibling, (p, flip(c, 1))))

    def scatter(part, landed):
        return plan(*[
            (part.at[flip(p, d)], landed.at[d - 1], (flip(p, d), c)) for d in range(1, 8)
        ])

    square_out = scatter(square_part, square_in)
    beside_out = scatter(beside_part, beside_in)
    cross_out = [scatter(cross_part.at[h], cross_in.at[h]) for h in range(2)]
    project_x = plan((project_part.at[1 - x], project_in_x, (flip(p, 1), c)))
    project_z = plan(*[
        (project_part.at[x, flip(z, d)], project_in_z.at[d - 1], (flip(z, d) * 2 + x, c))
        for d in range(1, 4)
    ])

    mine = early.at[k, x, z]
    early_z = plan(*[(mine, mine, (flip(z, d) * 2 + x, c)) for d in range(1, 4)])
    early_x = plan((early.at[k, x], early.at[k, x], (flip(p, 1), c)))
    early_core = plan((early.at[k], early.at[k], (p, flip(c, 1))))
    early_y = plan((early.at[k], other.at[k], (p, flip(c, 2))))
    other_core = plan((other.at[k], other.at[k], (p, flip(c, 1))))

    height = project_sum.shape[0] // 4

    def share(index):
        return project_sum.at[pl.ds(pl.multiple_of(index * height, height), height)]

    rhs_out = plan(*[
        (share(flip(c, d)), rhs_in.at[c], (p, flip(c, d))) for d in range(1, 4)
    ])
    depth = pair_in.shape[2]
    give = pl.ds(pl.multiple_of((1 - y) * depth, depth), depth)
    keep = pl.ds(pl.multiple_of(y * depth, depth), depth)
    pair_out = plan(
        (pair_sum.at[0, :, give], pair_in.at[0], (p, flip(c, 2))),
        (pair_sum.at[1, :, give], pair_in.at[1], (p, flip(c, 3))),
    )
    beside_x, beside_y, beside_core = (flip(p, 1), c), (p, flip(c, 2)), (p, flip(c, 1))

    def slot(side, across, d):
        return late.at[k, side, across, flip(z, d)]

    def send(ref, device):
        return plan((ref, ref, device))

    late_z = [
        send(slot(y, x, 0), (flip(z, d) * 2 + x, c)) for d in range(1, 4)
    ]
    late_x = [send(slot(y, x, d), beside_x) for d in range(4)]
    late_y = [send(slot(y, x, d), beside_y) for d in range(4)]
    late_on = [
        send(slot(1 - y, x, d), beside_x) if d % 2 else send(slot(y, 1 - x, d), beside_y)
        for d in range(4)
    ]
    late_core = [
        send(late.at[k, side, across], beside_core)
        for side, across in ((y, x), (y, 1 - x), (1 - y, x), (1 - y, 1 - x))
    ]

    def load(i, src, dst):
        return pltpu.make_async_copy(src, dst, local_sem.at[i])

    start(far[0])
    start(far[1])
    load(0, point_ref, own).start()
    start(beside)
    load(1, grid_ref, grid).start()

    def deal(part, value):
        step = value.shape[0] // 8
        for q in range(8):
            part[q] = value[q * step : (q + 1) * step]

    load(0, point_ref, own).wait()
    accumulate(total, lambda at: own[at, :], lambda at: own[at, :], 0, count)
    square = total[...]
    corner = jnp.concatenate([square[: mid // 2, :mid], square[mid // 2 : mid, :mid]], axis=1)
    deal(square_part, jnp.concatenate([square[mid:], corner], axis=0))
    start(square_out)

    arrive(beside)
    upper = total.at[pl.ds(0, mid)]

    @pl.when(k == 0)
    def _():
        accumulate(upper, lambda at: sibling[at, mid:], lambda at: own[at, :], 0, count)

    @pl.when(k == 1)
    def _():
        accumulate(upper, lambda at: own[at, :mid], lambda at: sibling[at, :], 0, count)

    deal(beside_part, upper[...])
    start(beside_out)

    load(1, grid_ref, grid).wait()
    tall = work.at[pl.ds(0, grid.shape[1]), pl.ds(0, width)]
    accumulate(tall, lambda at: grid[at, :], lambda at: own[at, :], 0, count)
    for q in range(8):
        project_part[q % 2, q // 2] = tall[q * 4 * height : (q + 1) * 4 * height, :]
    start(project_x)

    def gathered(value, landed):
        for d in range(landed.shape[0]):
            value = value + landed[d]
        return value

    cut = square_part.shape[1]
    arrive(square_out)
    mine[:cut] = gathered(square_part[p], square_in)
    arrive(beside_out)
    mine[cut:] = gathered(beside_part[p], beside_in)
    start(early_z)
    arrive(project_x)
    project_part[x] += project_in_x[...]
    start(project_z)
    arrive(early_z)
    start(early_x)

    def cross_terms(h):
        step = mid // 8
        for block, ours in ((0, own), (1, sibling)):
            def terms(flat, product):
                def chunk(i, carry):
                    there = pl.ds(pl.multiple_of(i * CHUNK, CHUNK), CHUNK)
                    here = pl.ds(
                        pl.multiple_of(y * (count // 2) + i * CHUNK, CHUNK), CHUNK
                    )
                    flat[...] += product(received[h, there, :], ours[here, :])
                    return carry

                flat[...] = jnp.zeros_like(flat)
                lax.fori_loop(0, count // 2 // CHUNK, chunk, 0)

            @pl.when(y == 0)
            def _():
                flat = total.at[pl.ds(0, mid), :]
                terms(flat, cross)
                for q in range(8):
                    cross_part[h, q, block] = flat[q * step : (q + 1) * step, :]

            @pl.when(y == 1)
            def _():
                flat = total.at[:, pl.ds(0, mid)]
                terms(flat, lambda there, here: cross(here, there))
                for q in range(8):
                    for part in range(2):
                        at = part * mid + q * step
                        cross_part[h, q, block, :, part * mid : (part + 1) * mid] = flat[
                            at : at + step, :
                        ]

        start(cross_out[h])

    arrive(far[0])
    cross_terms(0)
    arrive(early_x)
    start(early_core)
    arrive(project_z)
    project_sum[...] = gathered(project_part[x, z], project_in_z)
    start(rhs_out)
    rhs_in[c] = share(c)[...]
    arrive(early_core)

    def place(slots, at):
        def block(core, part):
            return jnp.concatenate([slots[core, q % 2, q // 2, part] for q in range(8)], axis=0)

        for core in range(2):
            lo = at + core * width
            held = block(core, slice(0, cut))
            work[lo + mid : lo + width, lo : lo + width] = held[:mid]
            work[lo : lo + mid // 2, lo : lo + mid] = held[mid:, :mid]
            work[lo + mid // 2 : lo + mid, lo : lo + mid] = held[mid:, mid:]
        lo, hi = at, at + width
        work[hi : hi + mid, lo:hi] = block(1, slice(cut, None))
        work[hi + mid : hi + width, lo:hi] = block(0, slice(cut, None))

    place(early, 0)

    def rest():
        arrive(far[1])
        start(early_y)
        cross_terms(1)

    def join():
        for h in range(2):
            arrive(cross_out[h])
            value = gathered(cross_part[h, p], cross_in.at[h])

            @pl.when(y == 0)
            def _():
                pair_sum[:, h] = value

            @pl.when(y == 1)
            def _():
                for part in range(2):
                    pair_sum[:, part, :, h * mid : (h + 1) * mid] = value[
                        :, :, part * mid : (part + 1) * mid
                    ]

        start(pair_out)
        arrive(early_y)
        start(other_core)
        arrive(rhs_out)
        for col in range(4):
            @pl.when(y == 0)
            def _():
                work[n : n + rows, col * width : (col + 1) * width] = rhs_in[col]

            @pl.when(y == 1)
            def _():
                work[n : n + rows, (col ^ 2) * width : ((col ^ 2) + 1) * width] = rhs_in[col]

        arrive(pair_out)
        late[k, y, x, z] = pair_sum[:, :, keep] + pair_in[...]
        for copies in late_z + [late_x[0], late_y[0]]:
            start(copies)
        arrive(other_core)
        place(other, half)
        for d in range(1, 4):
            arrive(late_z[d - 1])
            start(late_x[d])
            start(late_y[d])
        start(late_core[0])
        for d in range(4):
            arrive(late_x[d])
            arrive(late_y[d])
            start(late_on[d])
        start(late_core[1])
        start(late_core[2])
        for d in range(4):
            arrive(late_on[d])
        start(late_core[3])
        for copies in late_core:
            arrive(copies)
        for i in range(2):
            for j in range(2):
                pieces = []
                for part in range(2):
                    for q in range(8):
                        for side in range(2):
                            core = i if i == j or side == 0 else j
                            block = 0 if i == j else 1
                            pieces.append(late[core, side, q % 2, q // 2, block, part])
                value = jnp.concatenate(pieces, axis=0)

                @pl.when(y == 0)
                def _():
                    work[half + i * width : half + (i + 1) * width, j * width : (j + 1) * width] = value

                @pl.when(y == 1)
                def _():
                    work[half + j * width : half + (j + 1) * width, i * width : (i + 1) * width] = value.T

        limit = n + rows
        low = work[half:limit, :width]
        high = work[half:limit, width:half] - dot(low, work[width:half, :width], 1)
        low_ratio = dot(low, work[:width, :width])
        high_ratio = dot(high, work[width:half, width:half])
        for at in range(half, n, width):
            cut_at = at - half
            work[at:limit, at : at + width] -= dot(
                low_ratio[cut_at:], low[cut_at : cut_at + width], 1
            ) + dot(high_ratio[cut_at:], high[cut_at : cut_at + width], 1)
        work[half:limit, :width] = low_ratio
        work[half:limit, width:half] = high_ratio

    eliminate(work, inverse, n, rows, half, ((2, rest), (4, join)))
    solved = work.at[pl.ds(0, rows)]
    substitute(work, n, rows, solved)

    @pl.when(y == 0)
    def _():
        out_ref[...] = solved[...]

    @pl.when(y == 1)
    def _():
        out_ref[:, :half] = solved[:, half:]
        out_ref[:, half:] = solved[:, :half]

    for i, args in enumerate(used):
        copy(i, *args).wait_send()


def fused(point_values, grid_values):
    count, width = point_values.shape
    rows_all = grid_values.shape[1]
    n = 4 * width
    rows = rows_all // 32
    cut, side, deep = width * 3 // 32, width // 16, width // 16
    f32, bf16 = jnp.float32, jnp.bfloat16

    def buffer(*shape, dtype=f32):
        return pltpu.VMEM(shape, dtype)

    hbm = pl.BlockSpec(memory_space=pl.ANY)
    return pl.pallas_call(
        fused_kernel,
        out_shape=jax.ShapeDtypeStruct((rows, n), f32),
        in_specs=[hbm, hbm],
        out_specs=pl.BlockSpec(memory_space=pltpu.VMEM),
        scratch_shapes=[
            buffer(count, width, dtype=bf16),
            buffer(count, width, dtype=bf16),
            buffer(2, count // 2, width // 2, dtype=bf16),
            buffer(count, rows_all, dtype=bf16),
            buffer(width, width),
            buffer(8, cut, width),
            buffer(8, side, width),
            buffer(2, 4, rows_all // 8, width),
            buffer(2, 8, 2, deep, width),
            buffer(7, cut, width),
            buffer(7, side, width),
            buffer(4, rows_all // 8, width),
            buffer(3, rows_all // 8, width),
            buffer(2, 7, 2, deep, width),
            buffer(2, 2, deep, width),
            buffer(2, 2, deep // 2, width),
            buffer(rows_all // 8, width),
            buffer(4, rows, width),
            buffer(2, 2, 4, cut + side, width),
            buffer(2, 2, 4, cut + side, width),
            buffer(2, 2, 2, 4, 2, 2, deep // 2, width),
            buffer(n + rows, n),
            buffer(NB, NB),
            pltpu.SemaphoreType.DMA((2,)),
            pltpu.SemaphoreType.DMA((80,)),
            pltpu.SemaphoreType.DMA((80,)),
        ],
        compiler_params=pltpu.CompilerParams(
            collective_id=0, has_side_effects=True, vmem_limit_bytes=60 << 20
        ),
    )(point_values, grid_values)


def solution(mesh):
    cols, pairs = mesh.shape["col"], mesh.shape["pair"]

    def body(point_values, grid_values):
        if cols == 4 and pairs == 8:
            return fused(point_values, grid_values)
        project = cross(grid_values, point_values)
        gathered = lax.all_gather(point_values, "col", axis=1, tiled=True)
        gram = cross(gathered, point_values)
        width = gram.shape[1]
        both = jnp.concatenate(
            [gram.reshape(pairs, -1, width), project.reshape(pairs, -1, width)], axis=1
        )
        exchanged = lax.all_to_all(both, "pair", split_axis=0, concat_axis=0, tiled=True)
        own = jnp.sum(exchanged, axis=0)
        height = gram.shape[0] // pairs
        gram_parts = lax.all_gather(own[:height], ("pair", "col"), axis=0, tiled=False)
        regrouped = lax.all_to_all(own[height:], "col", split_axis=0, concat_axis=1, tiled=True)
        return solve(gram_parts, regrouped, cols)

    in_specs = (P("pair", "col"), P("pair", None))
    out_specs = P(("pair", "col"), None)
    return jax.shard_map(body, mesh=mesh, in_specs=in_specs, out_specs=out_specs, check_vma=False)
```

```python
import functools

import jax
import jax.numpy as jnp
from jax import lax
from jax.experimental import pallas as pl
from jax.experimental.pallas import tpu as pltpu
from jax.sharding import PartitionSpec as P

NB = 128
TILE = 8
PANEL = 16
CHUNK = 1024
MESH = pl.DeviceIdType.MESH


def cross(left, right):
    return lax.dot_general(
        left, right, (((0,), (0,)), ((), ())), preferred_element_type=jnp.float32
    )


def dot(left, right, over=0):
    return lax.dot_general(
        left, right, (((1,), (over,)), ((), ())),
        precision=lax.Precision.HIGHEST, preferred_element_type=jnp.float32,
    )


def invert(tiles):
    count, each = len(tiles), PANEL // TILE
    shape = tiles[0].shape
    lane = lax.broadcasted_iota(jnp.int32, shape, 1)
    sub = lax.broadcasted_iota(jnp.int32, shape, 0)

    def column(t, j):
        return jnp.broadcast_to(t[:, j : j + 1], shape)

    def row(t, s):
        return jnp.broadcast_to(t[s : s + 1, :], shape)

    tiles = list(tiles)
    for base in range(0, count, each):
        start = base * TILE
        group = range(base, base + each)
        cols = [[column(tiles[i], start + k) for i in group] for k in range(PANEL)]
        inside = (lane >= start) & (lane < start + PANEL)
        held = [
            jnp.where(inside, jnp.where(lane - i * TILE == sub, 1.0, 0.0), tiles[i])
            for i in group
        ]
        for k in range(PANEL):
            at, s = divmod(k, TILE)
            on_row = sub == s
            inv = 1.0 / row(cols[k][at], s)
            c = list(cols[k])
            c[at] = jnp.where(on_row, -1.0, c[at])

            def sweep(old):
                r = row(old[at], s) * inv
                old = list(old)
                old[at] = jnp.where(on_row, 0.0, old[at])
                return [old[a] - c[a] * r for a in range(each)]

            for m in range(k + 1, PANEL):
                cols[m] = sweep(cols[m])
            held = sweep(held)
        near = range(base + each, min(base + 2 * each, count))
        far = [i for i in range(count) if i not in group and i not in near]
        for i in near:
            part = [jnp.where(inside, 0.0, tiles[i]), jnp.zeros(shape, jnp.float32)]
            for k in range(PANEL):
                at, s = divmod(k, TILE)
                part[k % 2] -= column(tiles[i], start + k) * row(held[at], s)
            tiles[i] = part[0] + part[1]
        if far:
            left = jnp.concatenate([jnp.where(inside, tiles[i], 0.0) for i in far], axis=0)
            zero = jnp.zeros(shape, jnp.float32)
            right = jnp.concatenate(
                [held[i - base] if i in group else zero for i in range(count)], axis=0
            )
            product = dot(left, right)
            for q, i in enumerate(far):
                tiles[i] = jnp.where(inside, 0.0, tiles[i]) - product[q * TILE : (q + 1) * TILE]
        for i in group:
            tiles[i] = held[i - base]
    return tiles


def eliminate(work, inverse, n, rows, first=0, hooks=()):
    def step(k, carry):
        for at, hook in hooks:
            pl.when(k == at)(hook)
        for kk in range(n // NB):
            @pl.when(k == kk)
            def _():
                inverse[...] = work[kk * NB : (kk + 1) * NB, kk * NB : (kk + 1) * NB]

        tiles = invert([inverse[i : i + TILE, :] for i in range(0, NB, TILE)])
        for i, t in enumerate(tiles):
            inverse[i * TILE : (i + 1) * TILE, :] = t

        for kk in range(n // NB):
            lo = kk // 2 * 2 * NB
            mid, hi = lo + NB, lo + 2 * NB
            end, limit = (first, first) if lo < first else (n, n + rows)

            @pl.when(k == kk)
            def _():
                if kk % 2 == 0:
                    below = work[mid:hi, lo:mid]
                    scaled = dot(below, inverse[...])
                    work[mid:hi, lo:mid] = scaled
                    work[lo:mid, lo:mid] = inverse[...]
                    work[mid:hi, mid:hi] -= dot(scaled, below, 1)
                    return
                scaled = work[mid:hi, lo:mid]
                corner = dot(inverse[...], scaled)
                work[lo:mid, lo:mid] += dot(scaled.T, corner)
                work[lo:mid, mid:hi] = -corner.T
                work[mid:hi, lo:mid] = -corner
                work[mid:hi, mid:hi] = inverse[...]
                if hi == limit:
                    return
                below = work[hi:limit, lo:hi]
                ratio = dot(below, work[lo:hi, lo:hi])
                for at in range(hi, end, 2 * NB):
                    work[at:limit, at : at + 2 * NB] -= dot(
                        ratio[at - hi :], below[at - hi : at - hi + 2 * NB], 1
                    )
                work[hi:limit, lo:hi] = ratio
        return carry

    lax.fori_loop(0, n // NB, step, 0)


def substitute(work, n, rows, out_ref):
    for lo in range(n - 2 * NB, -1, -2 * NB):
        hi = lo + 2 * NB
        x = work[n : n + rows, lo:hi]
        if hi < n:
            x = x - dot(out_ref[:, hi:n], work[hi:n, lo:hi])
        out_ref[:, lo:hi] = x


def solve_kernel(cols, gram_ref, rhs_ref, out_ref, work, inverse):
    n = work.shape[1]
    rows = rhs_ref.shape[0]
    width = n // cols
    height = gram_ref.shape[1]
    for i in range(gram_ref.shape[0]):
        p, c = divmod(i, cols)
        work[p * height : (p + 1) * height, c * width : (c + 1) * width] = gram_ref[i]
    work[n : n + rows, :] = rhs_ref[...]
    eliminate(work, inverse, n, rows)
    substitute(work, n, rows, out_ref)


def solve(gram_parts, rhs, cols):
    rows, n = rhs.shape
    vmem = pl.BlockSpec(memory_space=pltpu.VMEM)
    return pl.pallas_call(
        functools.partial(solve_kernel, cols),
        out_shape=jax.ShapeDtypeStruct((rows, n), jnp.float32),
        in_specs=[vmem, vmem],
        out_specs=vmem,
        scratch_shapes=[
            pltpu.VMEM((n + rows, n), jnp.float32),
            pltpu.VMEM((NB, NB), jnp.float32),
        ],
        compiler_params=pltpu.CompilerParams(vmem_limit_bytes=48 << 20),
    )(gram_parts, rhs)


def flip(index, mask):
    total = 0
    for bit in (4, 2, 1):
        own = index // bit % 2
        total = total + bit * (1 - own if mask & bit else own)
    return total


def accumulate(total, left, right, start, count):
    total[...] = jnp.zeros_like(total)

    def chunk(i, carry):
        at = pl.ds(pl.multiple_of(start + i * CHUNK, CHUNK), CHUNK)
        total[...] += cross(left(at), right(at))
        return carry

    lax.fori_loop(0, count // CHUNK, chunk, 0)


def fused_kernel(
    point_ref, grid_ref, out_ref,
    own, sibling, received, grid, total, square_part, beside_part, project_part, cross_part,
    square_in, beside_in, project_in_x, project_in_z, cross_in, pair_sum, pair_in,
    project_sum, rhs_in,
    early, other, late, work, inverse, local_sem, send_sem, recv_sem,
):
    p, c = lax.axis_index("pair"), lax.axis_index("col")
    z, x, y, k = p // 2, p % 2, c // 2, c % 2
    count, width = own.shape
    n = work.shape[1]
    rows = out_ref.shape[0]
    mid, half = width // 2, n // 2

    barrier = pltpu.get_barrier_semaphore()
    friends = [(flip(p, d), c) for d in range(1, 8)] + [(p, flip(c, d)) for d in range(1, 4)]
    for friend in friends:
        pl.semaphore_signal(barrier, inc=1, device_id=friend, device_id_type=MESH)
    pl.semaphore_wait(barrier, len(friends))

    used = []

    def copy(at, src, dst, device):
        return pltpu.make_async_remote_copy(
            src_ref=src, dst_ref=dst, send_sem=send_sem.at[at], recv_sem=recv_sem.at[at],
            device_id=device, device_id_type=MESH,
        )

    def plan(*copies):
        base = len(used)
        used.extend(copies)
        return [functools.partial(copy, base + i, *args) for i, args in enumerate(copies)]

    def start(copies):
        for make in copies:
            make().start()

    def arrive(copies):
        for make in copies:
            make().wait_recv()

    away = pl.ds(pl.multiple_of((1 - y) * (count // 2), count // 2), count // 2)
    far = [
        plan((point_ref.at[away, pl.ds(h * mid, mid)], received.at[h], (p, flip(c, 2))))
        for h in range(2)
    ]
    beside = plan((point_ref, sibling, (p, flip(c, 1))))

    def scatter(part, landed):
        return plan(*[
            (part.at[flip(p, d)], landed.at[d - 1], (flip(p, d), c)) for d in range(1, 8)
        ])

    square_out = scatter(square_part, square_in)
    beside_out = scatter(beside_part, beside_in)
    cross_out = [scatter(cross_part.at[h], cross_in.at[h]) for h in range(2)]
    project_x = plan((project_part.at[1 - x], project_in_x, (flip(p, 1), c)))
    project_z = plan(*[
        (project_part.at[x, flip(z, d)], project_in_z.at[d - 1], (flip(z, d) * 2 + x, c))
        for d in range(1, 4)
    ])

    mine = early.at[k, x, z]
    early_z = plan(*[(mine, mine, (flip(z, d) * 2 + x, c)) for d in range(1, 4)])
    early_x = plan((early.at[k, x], early.at[k, x], (flip(p, 1), c)))
    early_core = plan((early.at[k], early.at[k], (p, flip(c, 1))))
    early_y = plan((early.at[k], other.at[k], (p, flip(c, 2))))
    other_core = plan((other.at[k], other.at[k], (p, flip(c, 1))))

    height = project_sum.shape[0] // 4

    def share(index):
        return project_sum.at[pl.ds(pl.multiple_of(index * height, height), height)]

    rhs_out = plan(*[
        (share(flip(c, d)), rhs_in.at[c], (p, flip(c, d))) for d in range(1, 4)
    ])
    depth = pair_in.shape[2]
    give = pl.ds(pl.multiple_of((1 - y) * depth, depth), depth)
    keep = pl.ds(pl.multiple_of(y * depth, depth), depth)
    pair_out = plan(
        (pair_sum.at[0, :, give], pair_in.at[0], (p, flip(c, 2))),
        (pair_sum.at[1, :, give], pair_in.at[1], (p, flip(c, 3))),
    )
    beside_x, beside_y, beside_core = (flip(p, 1), c), (p, flip(c, 2)), (p, flip(c, 1))

    def send(ref, device):
        return plan((ref, ref, device))

    late_z, late_x, late_y, late_on, late_core = [], [], [], [], []
    for block in range(2):
        piece = late.at[block, k]

        def slot(side, across, d):
            return piece.at[side, across, flip(z, d)]

        late_z.append([
            send(slot(y, x, 0), (flip(z, d) * 2 + x, c)) for d in range(1, 4)
        ])
        late_x.append([send(slot(y, x, d), beside_x) for d in range(4)])
        late_y.append([send(slot(y, x, d), beside_y) for d in range(4)])
        late_on.append([
            send(slot(1 - y, x, d), beside_x) if d % 2 else send(slot(y, 1 - x, d), beside_y)
            for d in range(4)
        ])
        late_core.append([
            send(piece.at[side, across], beside_core)
            for side, across in ((y, x), (y, 1 - x), (1 - y, x), (1 - y, 1 - x))
        ])

    def load(i, src, dst):
        return pltpu.make_async_copy(src, dst, local_sem.at[i])

    start(far[0])
    start(far[1])
    load(0, point_ref, own).start()
    start(beside)
    load(1, grid_ref, grid).start()

    def deal(part, value):
        step = value.shape[0] // 8
        for q in range(8):
            part[q] = value[q * step : (q + 1) * step]

    load(0, point_ref, own).wait()
    accumulate(total, lambda at: own[at, :], lambda at: own[at, :], 0, count)
    square = total[...]
    corner = jnp.concatenate([square[: mid // 2, :mid], square[mid // 2 : mid, :mid]], axis=1)
    deal(square_part, jnp.concatenate([square[mid:], corner], axis=0))
    start(square_out)

    arrive(beside)
    upper = total.at[pl.ds(0, mid)]

    @pl.when(k == 0)
    def _():
        accumulate(upper, lambda at: sibling[at, mid:], lambda at: own[at, :], 0, count)

    @pl.when(k == 1)
    def _():
        accumulate(upper, lambda at: own[at, :mid], lambda at: sibling[at, :], 0, count)

    deal(beside_part, upper[...])
    start(beside_out)

    load(1, grid_ref, grid).wait()
    tall = work.at[pl.ds(0, grid.shape[1]), pl.ds(0, width)]
    accumulate(tall, lambda at: grid[at, :], lambda at: own[at, :], 0, count)
    for q in range(8):
        project_part[q % 2, q // 2] = tall[q * 4 * height : (q + 1) * 4 * height, :]

    def gathered(value, landed):
        for d in range(landed.shape[0]):
            value = value + landed[d]
        return value

    cut = square_part.shape[1]
    arrive(square_out)
    mine[:cut] = gathered(square_part[p], square_in)
    arrive(beside_out)
    mine[cut:] = gathered(beside_part[p], beside_in)
    start(early_z)
    arrive(early_z)
    start(early_x)

    def cross_terms(h):
        step = mid // 8
        for block, ours in ((0, own), (1, sibling)):
            def terms(flat, product):
                def chunk(i, carry):
                    there = pl.ds(pl.multiple_of(i * CHUNK, CHUNK), CHUNK)
                    here = pl.ds(
                        pl.multiple_of(y * (count // 2) + i * CHUNK, CHUNK), CHUNK
                    )
                    flat[...] += product(received[h, there, :], ours[here, :])
                    return carry

                flat[...] = jnp.zeros_like(flat)
                lax.fori_loop(0, count // 2 // CHUNK, chunk, 0)

            @pl.when(y == 0)
            def _():
                flat = total.at[pl.ds(0, mid), :]
                terms(flat, cross)
                for q in range(8):
                    cross_part[h, q, block] = flat[q * step : (q + 1) * step, :]

            @pl.when(y == 1)
            def _():
                flat = total.at[:, pl.ds(0, mid)]
                terms(flat, lambda there, here: cross(here, there))
                for q in range(8):
                    for part in range(2):
                        at = part * mid + q * step
                        cross_part[h, q, block, :, part * mid : (part + 1) * mid] = flat[
                            at : at + step, :
                        ]

        start(cross_out[h])

    arrive(far[0])
    cross_terms(0)
    arrive(early_x)
    start(early_core)
    start(project_x)
    arrive(early_core)

    def place(slots, at):
        def block(core, part):
            return jnp.concatenate([slots[core, q % 2, q // 2, part] for q in range(8)], axis=0)

        for core in range(2):
            lo = at + core * width
            held = block(core, slice(0, cut))
            work[lo + mid : lo + width, lo : lo + width] = held[:mid]
            work[lo : lo + mid // 2, lo : lo + mid] = held[mid:, :mid]
            work[lo + mid // 2 : lo + mid, lo : lo + mid] = held[mid:, mid:]
        lo, hi = at, at + width
        work[hi : hi + mid, lo:hi] = block(1, slice(cut, None))
        work[hi + mid : hi + width, lo:hi] = block(0, slice(cut, None))

    place(early, 0)

    def project_terms():
        arrive(project_x)
        project_part[x] += project_in_x[...]
        start(project_z)

    def rest():
        arrive(far[1])
        start(early_y)
        cross_terms(1)

    def take(h):
        arrive(cross_out[h])
        value = gathered(cross_part[h, p], cross_in.at[h])

        @pl.when(y == 0)
        def _():
            pair_sum[:, h] = value

        @pl.when(y == 1)
        def _():
            for part in range(2):
                pair_sum[:, part, :, h * mid : (h + 1) * mid] = value[
                    :, :, part * mid : (part + 1) * mid
                ]

    def sums():
        arrive(project_z)
        project_sum[...] = gathered(project_part[x, z], project_in_z)
        start(rhs_out)
        rhs_in[c] = share(c)[...]
        take(0)

    def join():
        take(1)
        start(pair_out)
        arrive(early_y)
        start(other_core)
        arrive(rhs_out)
        for col in range(4):
            @pl.when(y == 0)
            def _():
                work[n : n + rows, col * width : (col + 1) * width] = rhs_in[col]

            @pl.when(y == 1)
            def _():
                work[n : n + rows, (col ^ 2) * width : ((col ^ 2) + 1) * width] = rhs_in[col]

        for block in range(2):
            arrive(pair_out[block : block + 1])
            late[block, k, y, x, z] = pair_sum[block, :, keep] + pair_in[block]
            for copies in late_z[block] + [late_x[block][0], late_y[block][0]]:
                start(copies)
        arrive(other_core)
        place(other, half)
        for block in range(2):
            for d in range(1, 4):
                arrive(late_z[block][d - 1])
                start(late_x[block][d])
                start(late_y[block][d])
            start(late_core[block][0])
        for block in range(2):
            for d in range(4):
                arrive(late_x[block][d])
                arrive(late_y[block][d])
                start(late_on[block][d])
            start(late_core[block][1])
            start(late_core[block][2])
        for block in range(2):
            for d in range(4):
                arrive(late_on[block][d])
            start(late_core[block][3])
        for block in range(2):
            for copies in late_core[block]:
                arrive(copies)
        for i in range(2):
            for j in range(2):
                pieces = []
                for part in range(2):
                    for q in range(8):
                        for side in range(2):
                            core = i if i == j or side == 0 else j
                            block = 0 if i == j else 1
                            pieces.append(late[block, core, side, q % 2, q // 2, part])
                value = jnp.concatenate(pieces, axis=0)

                @pl.when(y == 0)
                def _():
                    work[half + i * width : half + (i + 1) * width, j * width : (j + 1) * width] = value

                @pl.when(y == 1)
                def _():
                    work[half + j * width : half + (j + 1) * width, i * width : (i + 1) * width] = value.T

        limit = n + rows
        low = work[half:limit, :width]
        high = work[half:limit, width:half] - dot(low, work[width:half, :width], 1)
        low_ratio = dot(low, work[:width, :width])
        high_ratio = dot(high, work[width:half, width:half])
        for at in range(half, n, width):
            cut_at = at - half
            work[at:limit, at : at + width] -= dot(
                low_ratio[cut_at:], low[cut_at : cut_at + width], 1
            ) + dot(high_ratio[cut_at:], high[cut_at : cut_at + width], 1)
        work[half:limit, :width] = low_ratio
        work[half:limit, width:half] = high_ratio

    eliminate(work, inverse, n, rows, half, ((1, project_terms), (2, rest), (3, sums), (4, join)))
    solved = work.at[pl.ds(0, rows)]
    substitute(work, n, rows, solved)

    @pl.when(y == 0)
    def _():
        out_ref[...] = solved[...]

    @pl.when(y == 1)
    def _():
        out_ref[:, :half] = solved[:, half:]
        out_ref[:, half:] = solved[:, :half]

    for i, args in enumerate(used):
        copy(i, *args).wait_send()


def fused(point_values, grid_values):
    count, width = point_values.shape
    rows_all = grid_values.shape[1]
    n = 4 * width
    rows = rows_all // 32
    cut, side, deep = width * 3 // 32, width // 16, width // 16
    f32, bf16 = jnp.float32, jnp.bfloat16

    def buffer(*shape, dtype=f32):
        return pltpu.VMEM(shape, dtype)

    hbm = pl.BlockSpec(memory_space=pl.ANY)
    return pl.pallas_call(
        fused_kernel,
        out_shape=jax.ShapeDtypeStruct((rows, n), f32),
        in_specs=[hbm, hbm],
        out_specs=pl.BlockSpec(memory_space=pltpu.VMEM),
        scratch_shapes=[
            buffer(count, width, dtype=bf16),
            buffer(count, width, dtype=bf16),
            buffer(2, count // 2, width // 2, dtype=bf16),
            buffer(count, rows_all, dtype=bf16),
            buffer(width, width),
            buffer(8, cut, width),
            buffer(8, side, width),
            buffer(2, 4, rows_all // 8, width),
            buffer(2, 8, 2, deep, width),
            buffer(7, cut, width),
            buffer(7, side, width),
            buffer(4, rows_all // 8, width),
            buffer(3, rows_all // 8, width),
            buffer(2, 7, 2, deep, width),
            buffer(2, 2, deep, width),
            buffer(2, 2, deep // 2, width),
            buffer(rows_all // 8, width),
            buffer(4, rows, width),
            buffer(2, 2, 4, cut + side, width),
            buffer(2, 2, 4, cut + side, width),
            buffer(2, 2, 2, 2, 4, 2, deep // 2, width),
            buffer(n + rows, n),
            buffer(NB, NB),
            pltpu.SemaphoreType.DMA((2,)),
            pltpu.SemaphoreType.DMA((112,)),
            pltpu.SemaphoreType.DMA((112,)),
        ],
        compiler_params=pltpu.CompilerParams(
            collective_id=0, has_side_effects=True, vmem_limit_bytes=52 << 20
        ),
    )(point_values, grid_values)


def solution(mesh):
    cols, pairs = mesh.shape["col"], mesh.shape["pair"]

    def body(point_values, grid_values):
        if cols == 4 and pairs == 8:
            return fused(point_values, grid_values)
        project = cross(grid_values, point_values)
        gathered = lax.all_gather(point_values, "col", axis=1, tiled=True)
        gram = cross(gathered, point_values)
        width = gram.shape[1]
        both = jnp.concatenate(
            [gram.reshape(pairs, -1, width), project.reshape(pairs, -1, width)], axis=1
        )
        exchanged = lax.all_to_all(both, "pair", split_axis=0, concat_axis=0, tiled=True)
        own = jnp.sum(exchanged, axis=0)
        height = gram.shape[0] // pairs
        gram_parts = lax.all_gather(own[:height], ("pair", "col"), axis=0, tiled=False)
        regrouped = lax.all_to_all(own[height:], "col", split_axis=0, concat_axis=1, tiled=True)
        return solve(gram_parts, regrouped, cols)

    in_specs = (P("pair", "col"), P("pair", None))
    out_specs = P(("pair", "col"), None)
    return jax.shard_map(body, mesh=mesh, in_specs=in_specs, out_specs=out_specs, check_vma=False)
```

```python
import functools

import jax
import jax.numpy as jnp
from jax import lax
from jax.experimental import pallas as pl
from jax.experimental.pallas import tpu as pltpu
from jax.sharding import PartitionSpec as P

NB = 128
TILE = 8
PANEL = 16
CHUNK = 1024
MESH = pl.DeviceIdType.MESH


def cross(left, right):
    return lax.dot_general(
        left, right, (((0,), (0,)), ((), ())), preferred_element_type=jnp.float32
    )


def dot(left, right, over=0):
    return lax.dot_general(
        left, right, (((1,), (over,)), ((), ())),
        precision=lax.Precision.HIGHEST, preferred_element_type=jnp.float32,
    )


def invert(tiles):
    count, each = len(tiles), PANEL // TILE
    shape = tiles[0].shape
    lane = lax.broadcasted_iota(jnp.int32, shape, 1)
    sub = lax.broadcasted_iota(jnp.int32, shape, 0)

    def column(t, j):
        return jnp.broadcast_to(t[:, j : j + 1], shape)

    def row(t, s):
        return jnp.broadcast_to(t[s : s + 1, :], shape)

    tiles = list(tiles)
    for base in range(0, count, each):
        start = base * TILE
        group = range(base, base + each)
        cols = [[column(tiles[i], start + k) for i in group] for k in range(PANEL)]
        inside = (lane >= start) & (lane < start + PANEL)
        held = [
            jnp.where(inside, jnp.where(lane - i * TILE == sub, 1.0, 0.0), tiles[i])
            for i in group
        ]
        for k in range(PANEL):
            at, s = divmod(k, TILE)
            on_row = sub == s
            inv = 1.0 / row(cols[k][at], s)
            c = list(cols[k])
            c[at] = jnp.where(on_row, -1.0, c[at])

            def sweep(old):
                r = row(old[at], s) * inv
                old = list(old)
                old[at] = jnp.where(on_row, 0.0, old[at])
                return [old[a] - c[a] * r for a in range(each)]

            for m in range(k + 1, PANEL):
                cols[m] = sweep(cols[m])
            held = sweep(held)
        near = range(base + each, min(base + 2 * each, count))
        far = [i for i in range(count) if i not in group and i not in near]
        for i in near:
            part = [jnp.where(inside, 0.0, tiles[i]), jnp.zeros(shape, jnp.float32)]
            for k in range(PANEL):
                at, s = divmod(k, TILE)
                part[k % 2] -= column(tiles[i], start + k) * row(held[at], s)
            tiles[i] = part[0] + part[1]
        if far:
            left = jnp.concatenate([jnp.where(inside, tiles[i], 0.0) for i in far], axis=0)
            zero = jnp.zeros(shape, jnp.float32)
            right = jnp.concatenate(
                [held[i - base] if i in group else zero for i in range(count)], axis=0
            )
            product = dot(left, right)
            for q, i in enumerate(far):
                tiles[i] = jnp.where(inside, 0.0, tiles[i]) - product[q * TILE : (q + 1) * TILE]
        for i in group:
            tiles[i] = held[i - base]
    return tiles


def eliminate(work, inverse, n, rows, first=0, hooks=()):
    def step(k, carry):
        for at, hook in hooks:
            pl.when(k == at)(hook)
        for kk in range(n // NB):
            @pl.when(k == kk)
            def _():
                inverse[...] = work[kk * NB : (kk + 1) * NB, kk * NB : (kk + 1) * NB]

        tiles = invert([inverse[i : i + TILE, :] for i in range(0, NB, TILE)])
        for i, t in enumerate(tiles):
            inverse[i * TILE : (i + 1) * TILE, :] = t

        for kk in range(n // NB):
            lo = kk // 2 * 2 * NB
            mid, hi = lo + NB, lo + 2 * NB
            end, limit = (first, first) if lo < first else (n, n + rows)

            @pl.when(k == kk)
            def _():
                if kk % 2 == 0:
                    below = work[mid:hi, lo:mid]
                    scaled = dot(below, inverse[...])
                    work[mid:hi, lo:mid] = scaled
                    work[lo:mid, lo:mid] = inverse[...]
                    work[mid:hi, mid:hi] -= dot(scaled, below, 1)
                    return
                scaled = work[mid:hi, lo:mid]
                corner = dot(inverse[...], scaled)
                work[lo:mid, lo:mid] += dot(scaled.T, corner)
                work[lo:mid, mid:hi] = -corner.T
                work[mid:hi, lo:mid] = -corner
                work[mid:hi, mid:hi] = inverse[...]
                if hi == limit:
                    return
                below = work[hi:limit, lo:hi]
                ratio = dot(below, work[lo:hi, lo:hi])
                for at in range(hi, end, 2 * NB):
                    work[at:limit, at : at + 2 * NB] -= dot(
                        ratio[at - hi :], below[at - hi : at - hi + 2 * NB], 1
                    )
                work[hi:limit, lo:hi] = ratio
        return carry

    lax.fori_loop(0, n // NB, step, 0)


def substitute(work, n, rows, out_ref):
    for lo in range(n - 2 * NB, -1, -2 * NB):
        hi = lo + 2 * NB
        x = work[n : n + rows, lo:hi]
        if hi < n:
            x = x - dot(out_ref[:, hi:n], work[hi:n, lo:hi])
        out_ref[:, lo:hi] = x


def solve_kernel(cols, gram_ref, rhs_ref, out_ref, work, inverse):
    n = work.shape[1]
    rows = rhs_ref.shape[0]
    width = n // cols
    height = gram_ref.shape[1]
    for i in range(gram_ref.shape[0]):
        p, c = divmod(i, cols)
        work[p * height : (p + 1) * height, c * width : (c + 1) * width] = gram_ref[i]
    work[n : n + rows, :] = rhs_ref[...]
    eliminate(work, inverse, n, rows)
    substitute(work, n, rows, out_ref)


def solve(gram_parts, rhs, cols):
    rows, n = rhs.shape
    vmem = pl.BlockSpec(memory_space=pltpu.VMEM)
    return pl.pallas_call(
        functools.partial(solve_kernel, cols),
        out_shape=jax.ShapeDtypeStruct((rows, n), jnp.float32),
        in_specs=[vmem, vmem],
        out_specs=vmem,
        scratch_shapes=[
            pltpu.VMEM((n + rows, n), jnp.float32),
            pltpu.VMEM((NB, NB), jnp.float32),
        ],
        compiler_params=pltpu.CompilerParams(vmem_limit_bytes=48 << 20),
    )(gram_parts, rhs)


def flip(index, mask):
    total = 0
    for bit in (4, 2, 1):
        own = index // bit % 2
        total = total + bit * (1 - own if mask & bit else own)
    return total


def accumulate(total, left, right, start, count):
    total[...] = jnp.zeros_like(total)

    def chunk(i, carry):
        at = pl.ds(pl.multiple_of(start + i * CHUNK, CHUNK), CHUNK)
        total[...] += cross(left(at), right(at))
        return carry

    lax.fori_loop(0, count // CHUNK, chunk, 0)


def fused_kernel(
    point_ref, grid_ref, out_ref,
    own, sibling, received, grid, total, square_part, beside_part, project_part, cross_part,
    square_in, beside_in, project_in_x, project_in_z, cross_in, pair_sum, pair_in,
    project_sum, rhs_in,
    early, other, late, work, inverse, local_sem, send_sem, recv_sem,
):
    p, c = lax.axis_index("pair"), lax.axis_index("col")
    z, x, y, k = p // 2, p % 2, c // 2, c % 2
    count, width = own.shape
    n = work.shape[1]
    rows = out_ref.shape[0]
    mid, half = width // 2, n // 2

    barrier = pltpu.get_barrier_semaphore()
    friends = [(flip(p, d), c) for d in range(1, 8)] + [(p, flip(c, d)) for d in range(1, 4)]
    for friend in friends:
        pl.semaphore_signal(barrier, inc=1, device_id=friend, device_id_type=MESH)
    pl.semaphore_wait(barrier, len(friends))

    used = []

    def copy(at, src, dst, device):
        return pltpu.make_async_remote_copy(
            src_ref=src, dst_ref=dst, send_sem=send_sem.at[at], recv_sem=recv_sem.at[at],
            device_id=device, device_id_type=MESH,
        )

    def plan(*copies):
        base = len(used)
        used.extend(copies)
        return [functools.partial(copy, base + i, *args) for i, args in enumerate(copies)]

    def start(copies):
        for make in copies:
            make().start()

    def arrive(copies):
        for make in copies:
            make().wait_recv()

    away = pl.ds(pl.multiple_of((1 - y) * (count // 2), count // 2), count // 2)
    far = [
        plan((point_ref.at[away, pl.ds(h * mid, mid)], received.at[h], (p, flip(c, 2))))
        for h in range(2)
    ]
    beside = plan((point_ref, sibling, (p, flip(c, 1))))

    def scatter(part, landed):
        return plan(*[
            (part.at[flip(p, d)], landed.at[d - 1], (flip(p, d), c)) for d in range(1, 8)
        ])

    square_out = scatter(square_part, square_in)
    beside_out = scatter(beside_part, beside_in)
    cross_out = [scatter(cross_part.at[h], cross_in.at[h]) for h in range(2)]
    project_x = plan((project_part.at[1 - x], project_in_x, (flip(p, 1), c)))
    project_z = plan(*[
        (project_part.at[x, flip(z, d)], project_in_z.at[d - 1], (flip(z, d) * 2 + x, c))
        for d in range(1, 4)
    ])

    mine = early.at[k, x, z]
    early_z = plan(*[(mine, mine, (flip(z, d) * 2 + x, c)) for d in range(1, 4)])
    early_x = [
        plan((early.at[k, x, flip(z, d)], early.at[k, x, flip(z, d)], (flip(p, 1), c)))
        for d in range(4)
    ]
    early_core = plan((early.at[k], early.at[k], (p, flip(c, 1))))
    early_y = plan((early.at[k], other.at[k], (p, flip(c, 2))))
    other_core = plan((other.at[k], other.at[k], (p, flip(c, 1))))

    height = project_sum.shape[0] // 4

    def share(index):
        return project_sum.at[pl.ds(pl.multiple_of(index * height, height), height)]

    rhs_out = plan(*[
        (share(flip(c, d)), rhs_in.at[c], (p, flip(c, d))) for d in range(1, 4)
    ])
    depth = pair_in.shape[2]
    give = pl.ds(pl.multiple_of((1 - y) * depth, depth), depth)
    keep = pl.ds(pl.multiple_of(y * depth, depth), depth)
    pair_out = plan(
        (pair_sum.at[0, :, give], pair_in.at[0], (p, flip(c, 2))),
        (pair_sum.at[1, :, give], pair_in.at[1], (p, flip(c, 3))),
    )
    beside_x, beside_y, beside_core = (flip(p, 1), c), (p, flip(c, 2)), (p, flip(c, 1))

    def send(ref, device):
        return plan((ref, ref, device))

    late_z, late_x, late_y, late_on, late_core = [], [], [], [], []
    for block in range(2):
        piece = late.at[block, k]

        def slot(side, across, d):
            return piece.at[side, across, flip(z, d)]

        late_z.append([
            send(slot(y, x, 0), (flip(z, d) * 2 + x, c)) for d in range(1, 4)
        ])
        late_x.append([send(slot(y, x, d), beside_x) for d in range(4)])
        late_y.append([send(slot(y, x, d), beside_y) for d in range(4)])
        late_on.append([
            send(slot(1 - y, x, d), beside_x) if d % 2 else send(slot(y, 1 - x, d), beside_y)
            for d in range(4)
        ])
        late_core.append([
            send(piece.at[side, across], beside_core)
            for side, across in ((y, x), (y, 1 - x), (1 - y, x), (1 - y, 1 - x))
        ])

    def rows_of(i):
        return pl.ds(i * (count // 4), count // 4)

    def load(i, src, dst):
        return pltpu.make_async_copy(src, dst, local_sem.at[i])

    start(far[0])
    start(far[1])
    for i in range(4):
        load(i, point_ref.at[rows_of(i), :], own.at[rows_of(i), :]).start()
    start(beside)

    grid_load = load(4, grid_ref, grid)

    def deal(part, value):
        step = value.shape[0] // 8
        for q in range(8):
            part[q] = value[q * step : (q + 1) * step]

    for i in range(4):
        load(i, point_ref.at[rows_of(i), :], own.at[rows_of(i), :]).wait()
        square = cross(own[rows_of(i), :], own[rows_of(i), :])
        if i < 3:
            total[...] = square if i == 0 else total[...] + square
    square = total[...] + square
    corner = jnp.concatenate([square[: mid // 2, :mid], square[mid // 2 : mid, :mid]], axis=1)
    deal(square_part, jnp.concatenate([square[mid:], corner], axis=0))
    start(square_out)
    grid_load.start()

    arrive(beside)
    upper = total.at[pl.ds(0, mid)]

    @pl.when(k == 0)
    def _():
        accumulate(upper, lambda at: sibling[at, mid:], lambda at: own[at, :], 0, count)

    @pl.when(k == 1)
    def _():
        accumulate(upper, lambda at: own[at, :mid], lambda at: sibling[at, :], 0, count)

    deal(beside_part, upper[...])
    start(beside_out)

    grid_load.wait()
    tall = work.at[pl.ds(0, grid.shape[1]), pl.ds(0, width)]
    accumulate(tall, lambda at: grid[at, :], lambda at: own[at, :], 0, count)
    for q in range(8):
        project_part[q % 2, q // 2] = tall[q * 4 * height : (q + 1) * 4 * height, :]

    def gathered(value, landed):
        for d in range(landed.shape[0]):
            value = value + landed[d]
        return value

    cut = square_part.shape[1]
    arrive(square_out)
    mine[:cut] = gathered(square_part[p], square_in)
    arrive(beside_out)
    mine[cut:] = gathered(beside_part[p], beside_in)
    start(early_z)
    start(early_x[0])
    for d in range(1, 4):
        arrive(early_z[d - 1 : d])
        start(early_x[d])

    def cross_terms(h):
        step = mid // 8
        for block, ours in ((0, own), (1, sibling)):
            def terms(flat, product):
                def chunk(i, carry):
                    there = pl.ds(pl.multiple_of(i * CHUNK, CHUNK), CHUNK)
                    here = pl.ds(
                        pl.multiple_of(y * (count // 2) + i * CHUNK, CHUNK), CHUNK
                    )
                    flat[...] += product(received[h, there, :], ours[here, :])
                    return carry

                flat[...] = jnp.zeros_like(flat)
                lax.fori_loop(0, count // 2 // CHUNK, chunk, 0)

            @pl.when(y == 0)
            def _():
                flat = total.at[pl.ds(0, mid), :]
                terms(flat, cross)
                for q in range(8):
                    cross_part[h, q, block] = flat[q * step : (q + 1) * step, :]

            @pl.when(y == 1)
            def _():
                flat = total.at[:, pl.ds(0, mid)]
                terms(flat, lambda there, here: cross(here, there))
                for q in range(8):
                    for part in range(2):
                        at = part * mid + q * step
                        cross_part[h, q, block, :, part * mid : (part + 1) * mid] = flat[
                            at : at + step, :
                        ]

        start(cross_out[h])

    arrive(far[0])
    cross_terms(0)
    for copies in early_x:
        arrive(copies)
    start(early_core)
    start(project_x)
    arrive(early_core)

    def place(slots, at):
        def block(core, part):
            return jnp.concatenate([slots[core, q % 2, q // 2, part] for q in range(8)], axis=0)

        for core in range(2):
            lo = at + core * width
            held = block(core, slice(0, cut))
            work[lo + mid : lo + width, lo : lo + width] = held[:mid]
            work[lo : lo + mid // 2, lo : lo + mid] = held[mid:, :mid]
            work[lo + mid // 2 : lo + mid, lo : lo + mid] = held[mid:, mid:]
        lo, hi = at, at + width
        work[hi : hi + mid, lo:hi] = block(1, slice(cut, None))
        work[hi + mid : hi + width, lo:hi] = block(0, slice(cut, None))

    place(early, 0)

    def project_terms():
        arrive(project_x)
        project_part[x] += project_in_x[...]
        start(project_z)

    def rest():
        arrive(far[1])
        start(early_y)
        cross_terms(1)
        take(0)

    def take(h):
        arrive(cross_out[h])
        value = gathered(cross_part[h, p], cross_in.at[h])

        @pl.when(y == 0)
        def _():
            pair_sum[:, h] = value

        @pl.when(y == 1)
        def _():
            for part in range(2):
                pair_sum[:, part, :, h * mid : (h + 1) * mid] = value[
                    :, :, part * mid : (part + 1) * mid
                ]

    def sums():
        arrive(project_z)
        project_sum[...] = gathered(project_part[x, z], project_in_z)
        start(rhs_out)
        rhs_in[c] = share(c)[...]
        take(1)
        start(pair_out)

    def launch():
        for block in range(2):
            arrive(pair_out[block : block + 1])
            late[block, k, y, x, z] = pair_sum[block, :, keep] + pair_in[block]
            for copies in late_z[block] + [late_x[block][0], late_y[block][0]]:
                start(copies)
        arrive(early_y)
        start(other_core)

    def join():
        for block in range(2):
            for d in range(1, 4):
                arrive(late_z[block][d - 1])
                start(late_x[block][d])
                start(late_y[block][d])
            start(late_core[block][0])
        arrive(rhs_out)
        for col in range(4):
            @pl.when(y == 0)
            def _():
                work[n : n + rows, col * width : (col + 1) * width] = rhs_in[col]

            @pl.when(y == 1)
            def _():
                work[n : n + rows, (col ^ 2) * width : ((col ^ 2) + 1) * width] = rhs_in[col]

        arrive(other_core)
        place(other, half)
        for block in range(2):
            for d in range(4):
                arrive(late_x[block][d])
                arrive(late_y[block][d])
                start(late_on[block][d])
            start(late_core[block][1])
            start(late_core[block][2])
        for block in range(2):
            for d in range(4):
                arrive(late_on[block][d])
            start(late_core[block][3])
        for block in range(2):
            for copies in late_core[block]:
                arrive(copies)
        for i in range(2):
            for j in range(2):
                pieces = []
                for part in range(2):
                    for q in range(8):
                        for side in range(2):
                            core = i if i == j or side == 0 else j
                            block = 0 if i == j else 1
                            pieces.append(late[block, core, side, q % 2, q // 2, part])
                value = jnp.concatenate(pieces, axis=0)

                @pl.when(y == 0)
                def _():
                    work[half + i * width : half + (i + 1) * width, j * width : (j + 1) * width] = value

                @pl.when(y == 1)
                def _():
                    work[half + j * width : half + (j + 1) * width, i * width : (i + 1) * width] = value.T

        limit = n + rows
        low = work[half:limit, :width]
        high = work[half:limit, width:half] - dot(low, work[width:half, :width], 1)
        low_ratio = dot(low, work[:width, :width])
        high_ratio = dot(high, work[width:half, width:half])
        for at in range(half, n, width):
            cut_at = at - half
            work[at:limit, at : at + width] -= dot(
                low_ratio[cut_at:], low[cut_at : cut_at + width], 1
            ) + dot(high_ratio[cut_at:], high[cut_at : cut_at + width], 1)
        work[half:limit, :width] = low_ratio
        work[half:limit, width:half] = high_ratio

    eliminate(work, inverse, n, rows, half, ((0, rest), (1, project_terms), (2, sums), (3, launch), (4, join)))
    solved = work.at[pl.ds(0, rows)]
    substitute(work, n, rows, solved)

    @pl.when(y == 0)
    def _():
        out_ref[...] = solved[...]

    @pl.when(y == 1)
    def _():
        out_ref[:, :half] = solved[:, half:]
        out_ref[:, half:] = solved[:, :half]

    for i, args in enumerate(used):
        copy(i, *args).wait_send()


def fused(point_values, grid_values):
    count, width = point_values.shape
    rows_all = grid_values.shape[1]
    n = 4 * width
    rows = rows_all // 32
    cut, side, deep = width * 3 // 32, width // 16, width // 16
    f32, bf16 = jnp.float32, jnp.bfloat16

    def buffer(*shape, dtype=f32):
        return pltpu.VMEM(shape, dtype)

    hbm = pl.BlockSpec(memory_space=pl.ANY)
    return pl.pallas_call(
        fused_kernel,
        out_shape=jax.ShapeDtypeStruct((rows, n), f32),
        in_specs=[hbm, hbm],
        out_specs=pl.BlockSpec(memory_space=pltpu.VMEM),
        scratch_shapes=[
            buffer(count, width, dtype=bf16),
            buffer(count, width, dtype=bf16),
            buffer(2, count // 2, width // 2, dtype=bf16),
            buffer(count, rows_all, dtype=bf16),
            buffer(width, width),
            buffer(8, cut, width),
            buffer(8, side, width),
            buffer(2, 4, rows_all // 8, width),
            buffer(2, 8, 2, deep, width),
            buffer(7, cut, width),
            buffer(7, side, width),
            buffer(4, rows_all // 8, width),
            buffer(3, rows_all // 8, width),
            buffer(2, 7, 2, deep, width),
            buffer(2, 2, deep, width),
            buffer(2, 2, deep // 2, width),
            buffer(rows_all // 8, width),
            buffer(4, rows, width),
            buffer(2, 2, 4, cut + side, width),
            buffer(2, 2, 4, cut + side, width),
            buffer(2, 2, 2, 2, 4, 2, deep // 2, width),
            buffer(n + rows, n),
            buffer(NB, NB),
            pltpu.SemaphoreType.DMA((5,)),
            pltpu.SemaphoreType.DMA((112,)),
            pltpu.SemaphoreType.DMA((112,)),
        ],
        compiler_params=pltpu.CompilerParams(
            collective_id=0, has_side_effects=True, vmem_limit_bytes=52 << 20
        ),
    )(point_values, grid_values)


def solution(mesh):
    cols, pairs = mesh.shape["col"], mesh.shape["pair"]

    def body(point_values, grid_values):
        if cols == 4 and pairs == 8:
            return fused(point_values, grid_values)
        project = cross(grid_values, point_values)
        gathered = lax.all_gather(point_values, "col", axis=1, tiled=True)
        gram = cross(gathered, point_values)
        width = gram.shape[1]
        both = jnp.concatenate(
            [gram.reshape(pairs, -1, width), project.reshape(pairs, -1, width)], axis=1
        )
        exchanged = lax.all_to_all(both, "pair", split_axis=0, concat_axis=0, tiled=True)
        own = jnp.sum(exchanged, axis=0)
        height = gram.shape[0] // pairs
        gram_parts = lax.all_gather(own[:height], ("pair", "col"), axis=0, tiled=False)
        regrouped = lax.all_to_all(own[height:], "col", split_axis=0, concat_axis=1, tiled=True)
        return solve(gram_parts, regrouped, cols)

    in_specs = (P("pair", "col"), P("pair", None))
    out_specs = P(("pair", "col"), None)
    return jax.shard_map(body, mesh=mesh, in_specs=in_specs, out_specs=out_specs, check_vma=False)
```

```python
import functools

import jax
import jax.numpy as jnp
from jax import lax
from jax.experimental import pallas as pl
from jax.experimental.pallas import tpu as pltpu
from jax.sharding import PartitionSpec as P

NB = 128
TILE = 8
PANEL = 16
CHUNK = 1024
MESH = pl.DeviceIdType.MESH


def cross(left, right):
    return lax.dot_general(
        left, right, (((0,), (0,)), ((), ())), preferred_element_type=jnp.float32
    )


def dot(left, right, over=0):
    return lax.dot_general(
        left, right, (((1,), (over,)), ((), ())),
        precision=lax.Precision.HIGHEST, preferred_element_type=jnp.float32,
    )


def invert(tiles):
    count, each = len(tiles), PANEL // TILE
    shape = tiles[0].shape
    lane = lax.broadcasted_iota(jnp.int32, shape, 1)
    sub = lax.broadcasted_iota(jnp.int32, shape, 0)

    def column(t, j):
        return jnp.broadcast_to(t[:, j : j + 1], shape)

    def row(t, s):
        return jnp.broadcast_to(t[s : s + 1, :], shape)

    tiles = list(tiles)
    for base in range(0, count, each):
        start = base * TILE
        group = range(base, base + each)
        cols = [[column(tiles[i], start + k) for i in group] for k in range(PANEL)]
        inside = (lane >= start) & (lane < start + PANEL)
        held = [
            jnp.where(inside, jnp.where(lane - i * TILE == sub, 1.0, 0.0), tiles[i])
            for i in group
        ]
        for k in range(PANEL):
            at, s = divmod(k, TILE)
            on_row = sub == s
            inv = 1.0 / row(cols[k][at], s)
            c = list(cols[k])
            c[at] = jnp.where(on_row, -1.0, c[at])

            def sweep(old):
                r = row(old[at], s) * inv
                old = list(old)
                old[at] = jnp.where(on_row, 0.0, old[at])
                return [old[a] - c[a] * r for a in range(each)]

            for m in range(k + 1, PANEL):
                cols[m] = sweep(cols[m])
            held = sweep(held)
        near = range(base + each, min(base + 2 * each, count))
        far = [i for i in range(count) if i not in group and i not in near]
        for i in near:
            part = [jnp.where(inside, 0.0, tiles[i]), jnp.zeros(shape, jnp.float32)]
            for k in range(PANEL):
                at, s = divmod(k, TILE)
                part[k % 2] -= column(tiles[i], start + k) * row(held[at], s)
            tiles[i] = part[0] + part[1]
        if far:
            left = jnp.concatenate([jnp.where(inside, tiles[i], 0.0) for i in far], axis=0)
            zero = jnp.zeros(shape, jnp.float32)
            right = jnp.concatenate(
                [held[i - base] if i in group else zero for i in range(count)], axis=0
            )
            product = dot(left, right)
            for q, i in enumerate(far):
                tiles[i] = jnp.where(inside, 0.0, tiles[i]) - product[q * TILE : (q + 1) * TILE]
        for i in group:
            tiles[i] = held[i - base]
    return tiles


def eliminate(work, inverse, n, rows, first=0, hooks=()):
    def step(k, carry):
        for at, hook in hooks:
            pl.when(k == at)(hook)
        for kk in range((first or n) // NB):
            @pl.when(k == kk)
            def _():
                inverse[...] = work[kk * NB : (kk + 1) * NB, kk * NB : (kk + 1) * NB]

        tiles = invert([inverse[i : i + TILE, :] for i in range(0, NB, TILE)])
        for i, t in enumerate(tiles):
            inverse[i * TILE : (i + 1) * TILE, :] = t

        for kk in range((first or n) // NB):
            lo = kk // 2 * 2 * NB
            mid, hi = lo + NB, lo + 2 * NB
            end, limit = (first, first) if first else (n, n + rows)

            @pl.when(k == kk)
            def _():
                if kk % 2 == 0:
                    below = work[mid:hi, lo:mid]
                    scaled = dot(below, inverse[...])
                    work[mid:hi, lo:mid] = scaled
                    work[lo:mid, lo:mid] = inverse[...]
                    work[mid:hi, mid:hi] -= dot(scaled, below, 1)
                    return
                scaled = work[mid:hi, lo:mid]
                corner = dot(inverse[...], scaled)
                work[lo:mid, lo:mid] += dot(scaled.T, corner)
                work[lo:mid, mid:hi] = -corner.T
                work[mid:hi, lo:mid] = -corner
                work[mid:hi, mid:hi] = inverse[...]
                if hi == limit:
                    return
                below = work[hi:limit, lo:hi]
                ratio = dot(below, work[lo:hi, lo:hi])
                for at in range(hi, end, 2 * NB):
                    work[at:limit, at : at + 2 * NB] -= dot(
                        ratio[at - hi :], below[at - hi : at - hi + 2 * NB], 1
                    )
                work[hi:limit, lo:hi] = ratio
        return carry

    lax.fori_loop(0, (first or n) // NB, step, 0)


def finish(work, n, rows, first):
    blocks = (n - first) // NB
    count = range(blocks)

    def at(i):
        return slice(first + i * NB, first + (i + 1) * NB if i < blocks else n + rows)

    left = {(i, j): work[at(i), at(j)] for i in range(blocks + 1) for j in count if j <= i}
    ratio = {}
    for b in count:
        tiles = invert([left[b, b][i : i + TILE] for i in range(0, NB, TILE)])
        inv = jnp.concatenate(tiles, axis=0)
        for i in range(b + 1, blocks + 1):
            ratio[i, b] = dot(left[i, b], inv)
            for j in range(b + 1, min(i, blocks - 1) + 1):
                left[i, j] = left[i, j] - dot(ratio[i, b], left[j, b], 1)
    found = [None] * blocks
    for b in reversed(count):
        x = ratio[blocks, b]
        for i in range(b + 1, blocks):
            x = x - dot(found[i], ratio[i, b])
        found[b] = x
    far = jnp.concatenate(found, axis=1)
    near = work[n : n + rows, :first] - dot(far, work[first:n, :first])
    mid = first // 2
    high = near[:, mid:]
    low = near[:, :mid] - dot(high, work[mid:first, :mid])
    return jnp.concatenate([low, high], axis=1), far


def substitute(work, n, rows, out_ref):
    for lo in range(n - 2 * NB, -1, -2 * NB):
        hi = lo + 2 * NB
        x = work[n : n + rows, lo:hi]
        if hi < n:
            x = x - dot(out_ref[:, hi:n], work[hi:n, lo:hi])
        out_ref[:, lo:hi] = x


def solve_kernel(cols, gram_ref, rhs_ref, out_ref, work, inverse):
    n = work.shape[1]
    rows = rhs_ref.shape[0]
    width = n // cols
    height = gram_ref.shape[1]
    for i in range(gram_ref.shape[0]):
        p, c = divmod(i, cols)
        work[p * height : (p + 1) * height, c * width : (c + 1) * width] = gram_ref[i]
    work[n : n + rows, :] = rhs_ref[...]
    eliminate(work, inverse, n, rows)
    substitute(work, n, rows, out_ref)


def solve(gram_parts, rhs, cols):
    rows, n = rhs.shape
    vmem = pl.BlockSpec(memory_space=pltpu.VMEM)
    return pl.pallas_call(
        functools.partial(solve_kernel, cols),
        out_shape=jax.ShapeDtypeStruct((rows, n), jnp.float32),
        in_specs=[vmem, vmem],
        out_specs=vmem,
        scratch_shapes=[
            pltpu.VMEM((n + rows, n), jnp.float32),
            pltpu.VMEM((NB, NB), jnp.float32),
        ],
        compiler_params=pltpu.CompilerParams(vmem_limit_bytes=48 << 20),
    )(gram_parts, rhs)


def flip(index, mask):
    total = 0
    for bit in (4, 2, 1):
        own = index // bit % 2
        total = total + bit * (1 - own if mask & bit else own)
    return total


def accumulate(total, left, right, start, count):
    total[...] = jnp.zeros_like(total)

    def chunk(i, carry):
        at = pl.ds(pl.multiple_of(start + i * CHUNK, CHUNK), CHUNK)
        total[...] += cross(left(at), right(at))
        return carry

    lax.fori_loop(0, count // CHUNK, chunk, 0)


def fused_kernel(
    point_ref, grid_ref, out_ref,
    own, sibling, received, grid, total, square_part, beside_part, project_part, cross_part,
    square_in, beside_in, project_in_x, project_in_z, cross_in, pair_sum, pair_in,
    project_sum, rhs_in,
    early, other, late, work, inverse, local_sem, send_sem, recv_sem,
):
    p, c = lax.axis_index("pair"), lax.axis_index("col")
    z, x, y, k = p // 2, p % 2, c // 2, c % 2
    count, width = own.shape
    n = work.shape[1]
    rows = out_ref.shape[0]
    mid, half = width // 2, n // 2

    barrier = pltpu.get_barrier_semaphore()
    friends = [(flip(p, d), c) for d in range(1, 8)] + [(p, flip(c, d)) for d in range(1, 4)]
    for friend in friends:
        pl.semaphore_signal(barrier, inc=1, device_id=friend, device_id_type=MESH)
    pl.semaphore_wait(barrier, len(friends))

    used = []

    def copy(at, src, dst, device):
        return pltpu.make_async_remote_copy(
            src_ref=src, dst_ref=dst, send_sem=send_sem.at[at], recv_sem=recv_sem.at[at],
            device_id=device, device_id_type=MESH,
        )

    def plan(*copies):
        base = len(used)
        used.extend(copies)
        return [functools.partial(copy, base + i, *args) for i, args in enumerate(copies)]

    def start(copies):
        for make in copies:
            make().start()

    def arrive(copies):
        for make in copies:
            make().wait_recv()

    away = pl.ds(pl.multiple_of((1 - y) * (count // 2), count // 2), count // 2)
    far = [
        plan((point_ref.at[away, pl.ds(h * mid, mid)], received.at[h], (p, flip(c, 2))))
        for h in range(2)
    ]
    beside = plan((point_ref, sibling, (p, flip(c, 1))))

    def scatter(part, landed):
        return plan(*[
            (part.at[flip(p, d)], landed.at[d - 1], (flip(p, d), c)) for d in range(1, 8)
        ])

    square_out = scatter(square_part, square_in)
    beside_out = scatter(beside_part, beside_in)
    cross_out = [scatter(cross_part.at[h], cross_in.at[h]) for h in range(2)]
    project_x = plan((project_part.at[1 - x], project_in_x, (flip(p, 1), c)))
    project_z = plan(*[
        (project_part.at[x, flip(z, d)], project_in_z.at[d - 1], (flip(z, d) * 2 + x, c))
        for d in range(1, 4)
    ])

    mine = early.at[k, x, z]
    early_z = plan(*[(mine, mine, (flip(z, d) * 2 + x, c)) for d in range(1, 4)])
    early_x = [
        plan((early.at[k, x, flip(z, d)], early.at[k, x, flip(z, d)], (flip(p, 1), c)))
        for d in range(4)
    ]
    early_core = plan((early.at[k], early.at[k], (p, flip(c, 1))))
    early_y = plan((early.at[k], other.at[k], (p, flip(c, 2))))
    other_core = plan((other.at[k], other.at[k], (p, flip(c, 1))))

    height = project_sum.shape[0] // 4

    def share(index):
        return project_sum.at[pl.ds(pl.multiple_of(index * height, height), height)]

    rhs_out = plan(*[
        (share(flip(c, d)), rhs_in.at[c], (p, flip(c, d))) for d in range(1, 4)
    ])
    depth = pair_in.shape[2]
    give = pl.ds(pl.multiple_of((1 - y) * depth, depth), depth)
    keep = pl.ds(pl.multiple_of(y * depth, depth), depth)
    pair_out = plan(
        (pair_sum.at[0, :, give], pair_in.at[0], (p, flip(c, 2))),
        (pair_sum.at[1, :, give], pair_in.at[1], (p, flip(c, 3))),
    )
    beside_x, beside_y, beside_core = (flip(p, 1), c), (p, flip(c, 2)), (p, flip(c, 1))

    def send(ref, device):
        return plan((ref, ref, device))

    late_z, late_x, late_y, late_on, late_core = [], [], [], [], []
    for block in range(2):
        piece = late.at[block, k]

        def slot(side, across, d):
            return piece.at[side, across, flip(z, d)]

        late_z.append([
            send(slot(y, x, 0), (flip(z, d) * 2 + x, c)) for d in range(1, 4)
        ])
        late_x.append([send(slot(y, x, d), beside_x) for d in range(4)])
        late_y.append([send(slot(y, x, d), beside_y) for d in range(4)])
        late_on.append([
            send(slot(1 - y, x, d), beside_x) if d % 2 else send(slot(y, 1 - x, d), beside_y)
            for d in range(4)
        ])
        late_core.append([
            send(piece.at[side, across], beside_core)
            for side, across in ((y, x), (y, 1 - x), (1 - y, x), (1 - y, 1 - x))
        ])

    def rows_of(i):
        return pl.ds(i * (count // 4), count // 4)

    def load(i, src, dst):
        return pltpu.make_async_copy(src, dst, local_sem.at[i])

    start(far[0])
    start(far[1])
    for i in range(4):
        load(i, point_ref.at[rows_of(i), :], own.at[rows_of(i), :]).start()
    start(beside)

    grid_load = load(4, grid_ref, grid)

    def deal(part, value):
        step = value.shape[0] // 8
        for q in range(8):
            part[q] = value[q * step : (q + 1) * step]

    for i in range(4):
        load(i, point_ref.at[rows_of(i), :], own.at[rows_of(i), :]).wait()
        square = cross(own[rows_of(i), :], own[rows_of(i), :])
        if i < 3:
            total[...] = square if i == 0 else total[...] + square
    square = total[...] + square
    corner = jnp.concatenate([square[: mid // 2, :mid], square[mid // 2 : mid, :mid]], axis=1)
    deal(square_part, jnp.concatenate([square[mid:], corner], axis=0))
    start(square_out)
    grid_load.start()

    arrive(beside)
    upper = total.at[pl.ds(0, mid)]

    @pl.when(k == 0)
    def _():
        accumulate(upper, lambda at: sibling[at, mid:], lambda at: own[at, :], 0, count)

    @pl.when(k == 1)
    def _():
        accumulate(upper, lambda at: own[at, :mid], lambda at: sibling[at, :], 0, count)

    deal(beside_part, upper[...])
    start(beside_out)

    grid_load.wait()
    tall = work.at[pl.ds(0, grid.shape[1]), pl.ds(0, width)]
    accumulate(tall, lambda at: grid[at, :], lambda at: own[at, :], 0, count)
    for q in range(8):
        project_part[q % 2, q // 2] = tall[q * 4 * height : (q + 1) * 4 * height, :]

    def gathered(value, landed):
        for d in range(landed.shape[0]):
            value = value + landed[d]
        return value

    cut = square_part.shape[1]
    arrive(square_out)
    mine[:cut] = gathered(square_part[p], square_in)
    arrive(beside_out)
    mine[cut:] = gathered(beside_part[p], beside_in)
    start(early_z)
    start(early_x[0])
    for d in range(1, 4):
        arrive(early_z[d - 1 : d])
        start(early_x[d])

    def cross_terms(h):
        step = mid // 8
        for block, ours in ((0, own), (1, sibling)):
            def terms(flat, product):
                def chunk(i, carry):
                    there = pl.ds(pl.multiple_of(i * CHUNK, CHUNK), CHUNK)
                    here = pl.ds(
                        pl.multiple_of(y * (count // 2) + i * CHUNK, CHUNK), CHUNK
                    )
                    flat[...] += product(received[h, there, :], ours[here, :])
                    return carry

                flat[...] = jnp.zeros_like(flat)
                lax.fori_loop(0, count // 2 // CHUNK, chunk, 0)

            @pl.when(y == 0)
            def _():
                flat = total.at[pl.ds(0, mid), :]
                terms(flat, cross)
                for q in range(8):
                    cross_part[h, q, block] = flat[q * step : (q + 1) * step, :]

            @pl.when(y == 1)
            def _():
                flat = total.at[:, pl.ds(0, mid)]
                terms(flat, lambda there, here: cross(here, there))
                for q in range(8):
                    for part in range(2):
                        at = part * mid + q * step
                        cross_part[h, q, block, :, part * mid : (part + 1) * mid] = flat[
                            at : at + step, :
                        ]

        start(cross_out[h])

    arrive(far[0])
    cross_terms(0)
    for copies in early_x:
        arrive(copies)
    start(early_core)
    start(project_x)
    arrive(early_core)

    def place(slots, at):
        def block(core, part):
            return jnp.concatenate([slots[core, q % 2, q // 2, part] for q in range(8)], axis=0)

        for core in range(2):
            lo = at + core * width
            held = block(core, slice(0, cut))
            work[lo + mid : lo + width, lo : lo + width] = held[:mid]
            work[lo : lo + mid // 2, lo : lo + mid] = held[mid:, :mid]
            work[lo + mid // 2 : lo + mid, lo : lo + mid] = held[mid:, mid:]
        lo, hi = at, at + width
        work[hi : hi + mid, lo:hi] = block(1, slice(cut, None))
        work[hi + mid : hi + width, lo:hi] = block(0, slice(cut, None))

    place(early, 0)

    def project_terms():
        arrive(project_x)
        project_part[x] += project_in_x[...]
        start(project_z)

    def rest():
        arrive(far[1])
        start(early_y)
        cross_terms(1)
        take(0)

    def take(h):
        arrive(cross_out[h])
        value = gathered(cross_part[h, p], cross_in.at[h])

        @pl.when(y == 0)
        def _():
            pair_sum[:, h] = value

        @pl.when(y == 1)
        def _():
            for part in range(2):
                pair_sum[:, part, :, h * mid : (h + 1) * mid] = value[
                    :, :, part * mid : (part + 1) * mid
                ]

    def sums():
        arrive(project_z)
        project_sum[...] = gathered(project_part[x, z], project_in_z)
        start(rhs_out)
        rhs_in[c] = share(c)[...]
        take(1)
        start(pair_out)

    def launch():
        for block in range(2):
            arrive(pair_out[block : block + 1])
            late[block, k, y, x, z] = pair_sum[block, :, keep] + pair_in[block]
            for copies in late_z[block] + [late_x[block][0], late_y[block][0]]:
                start(copies)
        arrive(early_y)
        start(other_core)

    def join():
        for block in range(2):
            for d in range(1, 4):
                arrive(late_z[block][d - 1])
                start(late_x[block][d])
                start(late_y[block][d])
            start(late_core[block][0])
        arrive(rhs_out)
        for col in range(4):
            @pl.when(y == 0)
            def _():
                work[n : n + rows, col * width : (col + 1) * width] = rhs_in[col]

            @pl.when(y == 1)
            def _():
                work[n : n + rows, (col ^ 2) * width : ((col ^ 2) + 1) * width] = rhs_in[col]

        arrive(other_core)
        place(other, half)
        for block in range(2):
            for d in range(4):
                arrive(late_x[block][d])
                arrive(late_y[block][d])
                start(late_on[block][d])
            start(late_core[block][1])
            start(late_core[block][2])
        for block in range(2):
            for d in range(4):
                arrive(late_on[block][d])
            start(late_core[block][3])
        for block in range(2):
            for copies in late_core[block]:
                arrive(copies)
        for i in range(2):
            for j in range(2):
                pieces = []
                for part in range(2):
                    for q in range(8):
                        for side in range(2):
                            core = i if i == j or side == 0 else j
                            block = 0 if i == j else 1
                            pieces.append(late[block, core, side, q % 2, q // 2, part])
                value = jnp.concatenate(pieces, axis=0)

                @pl.when(y == 0)
                def _():
                    work[half + i * width : half + (i + 1) * width, j * width : (j + 1) * width] = value

                @pl.when(y == 1)
                def _():
                    work[half + j * width : half + (j + 1) * width, i * width : (i + 1) * width] = value.T

        limit = n + rows
        low = work[half:limit, :width]
        high = work[half:limit, width:half] - dot(low, work[width:half, :width], 1)
        low_ratio = dot(low, work[:width, :width])
        high_ratio = dot(high, work[width:half, width:half])
        for at in range(half, n, width):
            cut_at = at - half
            work[at:limit, at : at + width] -= dot(
                low_ratio[cut_at:], low[cut_at : cut_at + width], 1
            ) + dot(high_ratio[cut_at:], high[cut_at : cut_at + width], 1)
        work[half:limit, :width] = low_ratio
        work[half:limit, width:half] = high_ratio

    hooks = ((0, rest), (1, project_terms), (2, sums), (3, launch))
    eliminate(work, inverse, n, rows, half, hooks)
    join()
    near, far_side = finish(work, n, rows, half)

    @pl.when(y == 0)
    def _():
        out_ref[:, :half] = near
        out_ref[:, half:] = far_side

    @pl.when(y == 1)
    def _():
        out_ref[:, :half] = far_side
        out_ref[:, half:] = near

    for i, args in enumerate(used):
        copy(i, *args).wait_send()


def fused(point_values, grid_values):
    count, width = point_values.shape
    rows_all = grid_values.shape[1]
    n = 4 * width
    rows = rows_all // 32
    cut, side, deep = width * 3 // 32, width // 16, width // 16
    f32, bf16 = jnp.float32, jnp.bfloat16

    def buffer(*shape, dtype=f32):
        return pltpu.VMEM(shape, dtype)

    hbm = pl.BlockSpec(memory_space=pl.ANY)
    return pl.pallas_call(
        fused_kernel,
        out_shape=jax.ShapeDtypeStruct((rows, n), f32),
        in_specs=[hbm, hbm],
        out_specs=pl.BlockSpec(memory_space=pltpu.VMEM),
        scratch_shapes=[
            buffer(count, width, dtype=bf16),
            buffer(count, width, dtype=bf16),
            buffer(2, count // 2, width // 2, dtype=bf16),
            buffer(count, rows_all, dtype=bf16),
            buffer(width, width),
            buffer(8, cut, width),
            buffer(8, side, width),
            buffer(2, 4, rows_all // 8, width),
            buffer(2, 8, 2, deep, width),
            buffer(7, cut, width),
            buffer(7, side, width),
            buffer(4, rows_all // 8, width),
            buffer(3, rows_all // 8, width),
            buffer(2, 7, 2, deep, width),
            buffer(2, 2, deep, width),
            buffer(2, 2, deep // 2, width),
            buffer(rows_all // 8, width),
            buffer(4, rows, width),
            buffer(2, 2, 4, cut + side, width),
            buffer(2, 2, 4, cut + side, width),
            buffer(2, 2, 2, 2, 4, 2, deep // 2, width),
            buffer(n + rows, n),
            buffer(NB, NB),
            pltpu.SemaphoreType.DMA((5,)),
            pltpu.SemaphoreType.DMA((112,)),
            pltpu.SemaphoreType.DMA((112,)),
        ],
        compiler_params=pltpu.CompilerParams(
            collective_id=0, has_side_effects=True, vmem_limit_bytes=52 << 20
        ),
    )(point_values, grid_values)


def solution(mesh):
    cols, pairs = mesh.shape["col"], mesh.shape["pair"]

    def body(point_values, grid_values):
        if cols == 4 and pairs == 8:
            return fused(point_values, grid_values)
        project = cross(grid_values, point_values)
        gathered = lax.all_gather(point_values, "col", axis=1, tiled=True)
        gram = cross(gathered, point_values)
        width = gram.shape[1]
        both = jnp.concatenate(
            [gram.reshape(pairs, -1, width), project.reshape(pairs, -1, width)], axis=1
        )
        exchanged = lax.all_to_all(both, "pair", split_axis=0, concat_axis=0, tiled=True)
        own = jnp.sum(exchanged, axis=0)
        height = gram.shape[0] // pairs
        gram_parts = lax.all_gather(own[:height], ("pair", "col"), axis=0, tiled=False)
        regrouped = lax.all_to_all(own[height:], "col", split_axis=0, concat_axis=1, tiled=True)
        return solve(gram_parts, regrouped, cols)

    in_specs = (P("pair", "col"), P("pair", None))
    out_specs = P(("pair", "col"), None)
    return jax.shard_map(body, mesh=mesh, in_specs=in_specs, out_specs=out_specs, check_vma=False)
```

```python
import functools

import jax
import jax.numpy as jnp
from jax import lax
from jax.experimental import pallas as pl
from jax.experimental.pallas import tpu as pltpu
from jax.sharding import PartitionSpec as P

NB = 128
TILE = 8
PANEL = 16
CHUNK = 1024
MESH = pl.DeviceIdType.MESH


def cross(left, right):
    return lax.dot_general(
        left, right, (((0,), (0,)), ((), ())), preferred_element_type=jnp.float32
    )


def dot(left, right, over=0):
    return lax.dot_general(
        left, right, (((1,), (over,)), ((), ())),
        precision=lax.Precision.HIGHEST, preferred_element_type=jnp.float32,
    )


def invert(tiles):
    count, each = len(tiles), PANEL // TILE
    shape = tiles[0].shape
    lane = lax.broadcasted_iota(jnp.int32, shape, 1)
    sub = lax.broadcasted_iota(jnp.int32, shape, 0)

    def column(t, j):
        return jnp.broadcast_to(t[:, j : j + 1], shape)

    def row(t, s):
        return jnp.broadcast_to(t[s : s + 1, :], shape)

    tiles = list(tiles)
    for base in range(0, count, each):
        start = base * TILE
        group = range(base, base + each)
        cols = [[column(tiles[i], start + k) for i in group] for k in range(PANEL)]
        inside = (lane >= start) & (lane < start + PANEL)
        held = [
            jnp.where(inside, jnp.where(lane - i * TILE == sub, 1.0, 0.0), tiles[i])
            for i in group
        ]
        for k in range(PANEL):
            at, s = divmod(k, TILE)
            on_row = sub == s
            inv = 1.0 / row(cols[k][at], s)
            c = list(cols[k])
            c[at] = jnp.where(on_row, -1.0, c[at])

            def sweep(old):
                r = row(old[at], s) * inv
                old = list(old)
                old[at] = jnp.where(on_row, 0.0, old[at])
                return [old[a] - c[a] * r for a in range(each)]

            for m in range(k + 1, PANEL):
                cols[m] = sweep(cols[m])
            held = sweep(held)
        near = range(base + each, min(base + 2 * each, count))
        far = [i for i in range(count) if i not in group and i not in near]
        for i in near:
            part = [jnp.where(inside, 0.0, tiles[i]), jnp.zeros(shape, jnp.float32)]
            for k in range(PANEL):
                at, s = divmod(k, TILE)
                part[k % 2] -= column(tiles[i], start + k) * row(held[at], s)
            tiles[i] = part[0] + part[1]
        if far:
            left = jnp.concatenate([jnp.where(inside, tiles[i], 0.0) for i in far], axis=0)
            zero = jnp.zeros(shape, jnp.float32)
            right = jnp.concatenate(
                [held[i - base] if i in group else zero for i in range(count)], axis=0
            )
            product = dot(left, right)
            for q, i in enumerate(far):
                tiles[i] = jnp.where(inside, 0.0, tiles[i]) - product[q * TILE : (q + 1) * TILE]
        for i in group:
            tiles[i] = held[i - base]
    return tiles


def eliminate(work, inverse, n, rows, first=0, hooks=()):
    def step(k, carry):
        for at, hook in hooks:
            pl.when(k == at)(hook)
        for kk in range((first or n) // NB):
            @pl.when(k == kk)
            def _():
                inverse[...] = work[kk * NB : (kk + 1) * NB, kk * NB : (kk + 1) * NB]

        tiles = invert([inverse[i : i + TILE, :] for i in range(0, NB, TILE)])
        for i, t in enumerate(tiles):
            inverse[i * TILE : (i + 1) * TILE, :] = t

        for kk in range((first or n) // NB):
            lo = kk // 2 * 2 * NB
            mid, hi = lo + NB, lo + 2 * NB
            end, limit = (first, first) if first else (n, n + rows)

            @pl.when(k == kk)
            def _():
                if kk % 2 == 0:
                    below = work[mid:hi, lo:mid]
                    scaled = dot(below, inverse[...])
                    work[mid:hi, lo:mid] = scaled
                    work[lo:mid, lo:mid] = inverse[...]
                    work[mid:hi, mid:hi] -= dot(scaled, below, 1)
                    return
                scaled = work[mid:hi, lo:mid]
                corner = dot(inverse[...], scaled)
                work[lo:mid, lo:mid] += dot(scaled.T, corner)
                work[lo:mid, mid:hi] = -corner.T
                work[mid:hi, lo:mid] = -corner
                work[mid:hi, mid:hi] = inverse[...]
                if hi == limit:
                    return
                below = work[hi:limit, lo:hi]
                ratio = dot(below, work[lo:hi, lo:hi])
                for at in range(hi, end, 2 * NB):
                    work[at:limit, at : at + 2 * NB] -= dot(
                        ratio[at - hi :], below[at - hi : at - hi + 2 * NB], 1
                    )
                work[hi:limit, lo:hi] = ratio
        return carry

    lax.fori_loop(0, (first or n) // NB, step, 0)


def finish(work, n, rows, first):
    blocks = (n - first) // NB
    count = range(blocks)

    def at(i):
        return slice(first + i * NB, first + (i + 1) * NB if i < blocks else n + rows)

    left = {(i, j): work[at(i), at(j)] for i in range(blocks + 1) for j in count if j <= i}
    ratio = {}
    for b in count:
        tiles = invert([left[b, b][i : i + TILE] for i in range(0, NB, TILE)])
        inv = jnp.concatenate(tiles, axis=0)
        for i in range(b + 1, blocks + 1):
            ratio[i, b] = dot(left[i, b], inv)
            for j in range(b + 1, min(i, blocks - 1) + 1):
                left[i, j] = left[i, j] - dot(ratio[i, b], left[j, b], 1)
    found = [None] * blocks
    for b in reversed(count):
        x = ratio[blocks, b]
        for i in range(b + 1, blocks):
            x = x - dot(found[i], ratio[i, b])
        found[b] = x
    far = jnp.concatenate(found, axis=1)
    near = work[n : n + rows, :first] - dot(far, work[first:n, :first])
    mid = first // 2
    high = near[:, mid:]
    low = near[:, :mid] - dot(high, work[mid:first, :mid])
    return jnp.concatenate([low, high], axis=1), far


def substitute(work, n, rows, out_ref):
    for lo in range(n - 2 * NB, -1, -2 * NB):
        hi = lo + 2 * NB
        x = work[n : n + rows, lo:hi]
        if hi < n:
            x = x - dot(out_ref[:, hi:n], work[hi:n, lo:hi])
        out_ref[:, lo:hi] = x


def solve_kernel(cols, gram_ref, rhs_ref, out_ref, work, inverse):
    n = work.shape[1]
    rows = rhs_ref.shape[0]
    width = n // cols
    height = gram_ref.shape[1]
    for i in range(gram_ref.shape[0]):
        p, c = divmod(i, cols)
        work[p * height : (p + 1) * height, c * width : (c + 1) * width] = gram_ref[i]
    work[n : n + rows, :] = rhs_ref[...]
    eliminate(work, inverse, n, rows)
    substitute(work, n, rows, out_ref)


def solve(gram_parts, rhs, cols):
    rows, n = rhs.shape
    vmem = pl.BlockSpec(memory_space=pltpu.VMEM)
    return pl.pallas_call(
        functools.partial(solve_kernel, cols),
        out_shape=jax.ShapeDtypeStruct((rows, n), jnp.float32),
        in_specs=[vmem, vmem],
        out_specs=vmem,
        scratch_shapes=[
            pltpu.VMEM((n + rows, n), jnp.float32),
            pltpu.VMEM((NB, NB), jnp.float32),
        ],
        compiler_params=pltpu.CompilerParams(vmem_limit_bytes=48 << 20),
    )(gram_parts, rhs)


def flip(index, mask):
    total = 0
    for bit in (4, 2, 1):
        own = index // bit % 2
        total = total + bit * (1 - own if mask & bit else own)
    return total


def accumulate(total, left, right, start, count):
    total[...] = jnp.zeros_like(total)

    def chunk(i, carry):
        at = pl.ds(pl.multiple_of(start + i * CHUNK, CHUNK), CHUNK)
        total[...] += cross(left(at), right(at))
        return carry

    lax.fori_loop(0, count // CHUNK, chunk, 0)


def fused_kernel(
    point_ref, grid_ref, out_ref,
    own, sibling, received, grid, total, square_part, beside_part, project_part, cross_part,
    square_in, beside_in, project_in_x, project_in_z, cross_in, pair_sum, pair_in,
    project_sum, rhs_in,
    early, other, late, work, inverse, local_sem, send_sem, recv_sem,
):
    p, c = lax.axis_index("pair"), lax.axis_index("col")
    z, x, y, k = p // 2, p % 2, c // 2, c % 2
    count, width = own.shape
    n = work.shape[1]
    rows = out_ref.shape[0]
    mid, half = width // 2, n // 2

    barrier = pltpu.get_barrier_semaphore()
    friends = [(flip(p, d), c) for d in range(1, 8)] + [(p, flip(c, d)) for d in range(1, 4)]
    for friend in friends:
        pl.semaphore_signal(barrier, inc=1, device_id=friend, device_id_type=MESH)
    pl.semaphore_wait(barrier, len(friends))

    used = []

    def copy(at, src, dst, device):
        return pltpu.make_async_remote_copy(
            src_ref=src, dst_ref=dst, send_sem=send_sem.at[at], recv_sem=recv_sem.at[at],
            device_id=device, device_id_type=MESH,
        )

    def plan(*copies):
        base = len(used)
        used.extend(copies)
        return [functools.partial(copy, base + i, *args) for i, args in enumerate(copies)]

    def start(copies):
        for make in copies:
            make().start()

    def arrive(copies):
        for make in copies:
            make().wait_recv()

    away = pl.ds(pl.multiple_of((1 - y) * (count // 2), count // 2), count // 2)
    far = [
        plan((point_ref.at[away, pl.ds(h * mid, mid)], received.at[h], (p, flip(c, 2))))
        for h in range(2)
    ]
    beside = plan((point_ref, sibling, (p, flip(c, 1))))

    def scatter(part, landed):
        return plan(*[
            (part.at[flip(p, d)], landed.at[d - 1], (flip(p, d), c)) for d in range(1, 8)
        ])

    square_out = scatter(square_part, square_in)
    beside_out = scatter(beside_part, beside_in)
    cross_out = [scatter(cross_part.at[h], cross_in.at[h]) for h in range(2)]
    project_x = plan((project_part.at[1 - x], project_in_x, (flip(p, 1), c)))
    project_z = plan(*[
        (project_part.at[x, flip(z, d)], project_in_z.at[d - 1], (flip(z, d) * 2 + x, c))
        for d in range(1, 4)
    ])

    mine = early.at[k, x, z]
    early_z = plan(*[(mine, mine, (flip(z, d) * 2 + x, c)) for d in range(1, 4)])
    early_x = [
        plan((early.at[k, x, flip(z, d)], early.at[k, x, flip(z, d)], (flip(p, 1), c)))
        for d in range(4)
    ]
    early_core = plan((early.at[k], early.at[k], (p, flip(c, 1))))
    early_y = plan((early.at[k], other.at[k], (p, flip(c, 2))))
    other_core = plan((other.at[k], other.at[k], (p, flip(c, 1))))

    height = project_sum.shape[0] // 4

    def share(index):
        return project_sum.at[pl.ds(pl.multiple_of(index * height, height), height)]

    rhs_out = plan(*[
        (share(flip(c, d)), rhs_in.at[c], (p, flip(c, d))) for d in range(1, 4)
    ])
    depth = pair_in.shape[2]
    give = pl.ds(pl.multiple_of((1 - y) * depth, depth), depth)
    keep = pl.ds(pl.multiple_of(y * depth, depth), depth)
    pair_out = plan(
        (pair_sum.at[0, :, give], pair_in.at[0], (p, flip(c, 2))),
        (pair_sum.at[1, :, give], pair_in.at[1], (p, flip(c, 3))),
    )
    beside_x, beside_y, beside_core = (flip(p, 1), c), (p, flip(c, 2)), (p, flip(c, 1))

    def send(ref, device):
        return plan((ref, ref, device))

    late_z, late_x, late_y, late_on, late_core = [], [], [], [], []
    for block in range(2):
        piece = late.at[block, k]

        def slot(side, across, d):
            return piece.at[side, across, flip(z, d)]

        late_z.append([
            send(slot(y, x, 0), (flip(z, d) * 2 + x, c)) for d in range(1, 4)
        ])
        late_x.append([send(slot(y, x, d), beside_x) for d in range(4)])
        late_y.append([send(slot(y, x, d), beside_y) for d in range(4)])
        late_on.append([
            send(slot(1 - y, x, d), beside_x) if d % 2 else send(slot(y, 1 - x, d), beside_y)
            for d in range(4)
        ])
        late_core.append([
            send(piece.at[side, across], beside_core)
            for side, across in ((y, x), (y, 1 - x), (1 - y, x), (1 - y, 1 - x))
        ])

    def rows_of(i):
        return pl.ds(i * (count // 4), count // 4)

    def load(i, src, dst):
        return pltpu.make_async_copy(src, dst, local_sem.at[i])

    start(far[0])
    start(far[1])
    for i in range(4):
        load(i, point_ref.at[rows_of(i), :], own.at[rows_of(i), :]).start()
    start(beside)

    grid_load = load(4, grid_ref, grid)

    def deal(part, value):
        step = value.shape[0] // 8
        for q in range(8):
            part[q] = value[q * step : (q + 1) * step]

    for i in range(4):
        load(i, point_ref.at[rows_of(i), :], own.at[rows_of(i), :]).wait()
        square = cross(own[rows_of(i), :], own[rows_of(i), :])
        if i < 3:
            total[...] = square if i == 0 else total[...] + square
    square = total[...] + square
    corner = jnp.concatenate([square[: mid // 2, :mid], square[mid // 2 : mid, :mid]], axis=1)
    deal(square_part, jnp.concatenate([square[mid:], corner], axis=0))
    start(square_out)
    grid_load.start()

    arrive(beside)
    upper = total.at[pl.ds(0, mid)]

    @pl.when(k == 0)
    def _():
        accumulate(upper, lambda at: sibling[at, mid:], lambda at: own[at, :], 0, count)

    @pl.when(k == 1)
    def _():
        accumulate(upper, lambda at: own[at, :mid], lambda at: sibling[at, :], 0, count)

    deal(beside_part, upper[...])
    start(beside_out)

    grid_load.wait()
    tall = work.at[pl.ds(0, grid.shape[1]), pl.ds(0, width)]
    accumulate(tall, lambda at: grid[at, :], lambda at: own[at, :], 0, count)
    for q in range(8):
        project_part[q % 2, q // 2] = tall[q * 4 * height : (q + 1) * 4 * height, :]

    def gathered(value, landed):
        for d in range(landed.shape[0]):
            value = value + landed[d]
        return value

    cut = square_part.shape[1]
    arrive(square_out)
    mine[:cut] = gathered(square_part[p], square_in)
    arrive(beside_out)
    mine[cut:] = gathered(beside_part[p], beside_in)
    start(early_z)
    start(early_x[0])
    for d in range(1, 4):
        arrive(early_z[d - 1 : d])
        start(early_x[d])

    def cross_terms(h):
        step = mid // 8
        for block, ours in ((0, own), (1, sibling)):
            def terms(flat, product):
                def chunk(i, carry):
                    there = pl.ds(pl.multiple_of(i * CHUNK, CHUNK), CHUNK)
                    here = pl.ds(
                        pl.multiple_of(y * (count // 2) + i * CHUNK, CHUNK), CHUNK
                    )
                    flat[...] += product(received[h, there, :], ours[here, :])
                    return carry

                flat[...] = jnp.zeros_like(flat)
                lax.fori_loop(0, count // 2 // CHUNK, chunk, 0)

            @pl.when(y == 0)
            def _():
                flat = total.at[pl.ds(0, mid), :]
                terms(flat, cross)
                for q in range(8):
                    cross_part[h, q, block] = flat[q * step : (q + 1) * step, :]

            @pl.when(y == 1)
            def _():
                flat = total.at[:, pl.ds(0, mid)]
                terms(flat, lambda there, here: cross(here, there))
                for q in range(8):
                    for part in range(2):
                        at = part * mid + q * step
                        cross_part[h, q, block, :, part * mid : (part + 1) * mid] = flat[
                            at : at + step, :
                        ]

        start(cross_out[h])

    arrive(far[0])
    cross_terms(0)
    for copies in early_x:
        arrive(copies)
    start(early_core)
    start(project_x)
    arrive(early_core)

    def place(slots, at):
        def block(core, part):
            return jnp.concatenate([slots[core, q % 2, q // 2, part] for q in range(8)], axis=0)

        for core in range(2):
            lo = at + core * width
            held = block(core, slice(0, cut))
            work[lo + mid : lo + width, lo : lo + width] = held[:mid]
            work[lo : lo + mid // 2, lo : lo + mid] = held[mid:, :mid]
            work[lo + mid // 2 : lo + mid, lo : lo + mid] = held[mid:, mid:]
        lo, hi = at, at + width
        work[hi : hi + mid, lo:hi] = block(1, slice(cut, None))
        work[hi + mid : hi + width, lo:hi] = block(0, slice(cut, None))

    place(early, 0)

    def project_terms():
        arrive(project_x)
        project_part[x] += project_in_x[...]
        start(project_z)

    def rest():
        arrive(far[1])
        start(early_y)
        cross_terms(1)
        take(0)

    def take(h):
        arrive(cross_out[h])
        value = gathered(cross_part[h, p], cross_in.at[h])

        @pl.when(y == 0)
        def _():
            pair_sum[:, h] = value

        @pl.when(y == 1)
        def _():
            for part in range(2):
                pair_sum[:, part, :, h * mid : (h + 1) * mid] = value[
                    :, :, part * mid : (part + 1) * mid
                ]

    def sums():
        take(1)
        start(pair_out)
        for block in range(2):
            arrive(pair_out[block : block + 1])
            late[block, k, y, x, z] = pair_sum[block, :, keep] + pair_in[block]
            for copies in late_z[block] + [late_x[block][0], late_y[block][0]]:
                start(copies)

    def spread():
        for block in range(2):
            for d in range(1, 4):
                arrive(late_z[block][d - 1])
                start(late_x[block][d])
                start(late_y[block][d])
            start(late_core[block][0])
        arrive(early_y)
        start(other_core)
        arrive(project_z)
        project_sum[...] = gathered(project_part[x, z], project_in_z)
        start(rhs_out)
        rhs_in[c] = share(c)[...]

    def join():
        for block in range(2):
            for d in range(4):
                arrive(late_x[block][d])
                arrive(late_y[block][d])
                start(late_on[block][d])
            start(late_core[block][1])
            start(late_core[block][2])
        arrive(rhs_out)
        for col in range(4):
            @pl.when(y == 0)
            def _():
                work[n : n + rows, col * width : (col + 1) * width] = rhs_in[col]

            @pl.when(y == 1)
            def _():
                work[n : n + rows, (col ^ 2) * width : ((col ^ 2) + 1) * width] = rhs_in[col]

        arrive(other_core)
        place(other, half)
        for block in range(2):
            for d in range(4):
                arrive(late_on[block][d])
            start(late_core[block][3])
        for block in range(2):
            for copies in late_core[block]:
                arrive(copies)
        for i in range(2):
            for j in range(2):
                pieces = []
                for part in range(2):
                    for q in range(8):
                        for side in range(2):
                            core = i if i == j or side == 0 else j
                            block = 0 if i == j else 1
                            pieces.append(late[block, core, side, q % 2, q // 2, part])
                value = jnp.concatenate(pieces, axis=0)

                @pl.when(y == 0)
                def _():
                    work[half + i * width : half + (i + 1) * width, j * width : (j + 1) * width] = value

                @pl.when(y == 1)
                def _():
                    work[half + j * width : half + (j + 1) * width, i * width : (i + 1) * width] = value.T

        limit = n + rows
        low = work[half:limit, :width]
        high = work[half:limit, width:half] - dot(low, work[width:half, :width], 1)
        both = jnp.concatenate([low, high], axis=1)
        ratio = jnp.concatenate(
            [dot(low, work[:width, :width]), dot(high, work[width:half, width:half])], axis=1
        )
        for at in range(half, n, width):
            work[at:limit, at : at + width] -= dot(
                ratio[at - half :], both[at - half : at - half + width], 1
            )
        work[half:limit, :half] = ratio

    hooks = ((0, rest), (1, project_terms), (2, sums), (3, spread))
    eliminate(work, inverse, n, rows, half, hooks)
    join()
    near, far_side = finish(work, n, rows, half)

    @pl.when(y == 0)
    def _():
        out_ref[:, :half] = near
        out_ref[:, half:] = far_side

    @pl.when(y == 1)
    def _():
        out_ref[:, :half] = far_side
        out_ref[:, half:] = near

    for i, args in enumerate(used):
        copy(i, *args).wait_send()


def fused(point_values, grid_values):
    count, width = point_values.shape
    rows_all = grid_values.shape[1]
    n = 4 * width
    rows = rows_all // 32
    cut, side, deep = width * 3 // 32, width // 16, width // 16
    f32, bf16 = jnp.float32, jnp.bfloat16

    def buffer(*shape, dtype=f32):
        return pltpu.VMEM(shape, dtype)

    hbm = pl.BlockSpec(memory_space=pl.ANY)
    return pl.pallas_call(
        fused_kernel,
        out_shape=jax.ShapeDtypeStruct((rows, n), f32),
        in_specs=[hbm, hbm],
        out_specs=pl.BlockSpec(memory_space=pltpu.VMEM),
        scratch_shapes=[
            buffer(count, width, dtype=bf16),
            buffer(count, width, dtype=bf16),
            buffer(2, count // 2, width // 2, dtype=bf16),
            buffer(count, rows_all, dtype=bf16),
            buffer(width, width),
            buffer(8, cut, width),
            buffer(8, side, width),
            buffer(2, 4, rows_all // 8, width),
            buffer(2, 8, 2, deep, width),
            buffer(7, cut, width),
            buffer(7, side, width),
            buffer(4, rows_all // 8, width),
            buffer(3, rows_all // 8, width),
            buffer(2, 7, 2, deep, width),
            buffer(2, 2, deep, width),
            buffer(2, 2, deep // 2, width),
            buffer(rows_all // 8, width),
            buffer(4, rows, width),
            buffer(2, 2, 4, cut + side, width),
            buffer(2, 2, 4, cut + side, width),
            buffer(2, 2, 2, 2, 4, 2, deep // 2, width),
            buffer(n + rows, n),
            buffer(NB, NB),
            pltpu.SemaphoreType.DMA((5,)),
            pltpu.SemaphoreType.DMA((112,)),
            pltpu.SemaphoreType.DMA((112,)),
        ],
        compiler_params=pltpu.CompilerParams(
            collective_id=0, has_side_effects=True, vmem_limit_bytes=52 << 20
        ),
    )(point_values, grid_values)


def solution(mesh):
    cols, pairs = mesh.shape["col"], mesh.shape["pair"]

    def body(point_values, grid_values):
        if cols == 4 and pairs == 8:
            return fused(point_values, grid_values)
        project = cross(grid_values, point_values)
        gathered = lax.all_gather(point_values, "col", axis=1, tiled=True)
        gram = cross(gathered, point_values)
        width = gram.shape[1]
        both = jnp.concatenate(
            [gram.reshape(pairs, -1, width), project.reshape(pairs, -1, width)], axis=1
        )
        exchanged = lax.all_to_all(both, "pair", split_axis=0, concat_axis=0, tiled=True)
        own = jnp.sum(exchanged, axis=0)
        height = gram.shape[0] // pairs
        gram_parts = lax.all_gather(own[:height], ("pair", "col"), axis=0, tiled=False)
        regrouped = lax.all_to_all(own[height:], "col", split_axis=0, concat_axis=1, tiled=True)
        return solve(gram_parts, regrouped, cols)

    in_specs = (P("pair", "col"), P("pair", None))
    out_specs = P(("pair", "col"), None)
    return jax.shard_map(body, mesh=mesh, in_specs=in_specs, out_specs=out_specs, check_vma=False)
```

```python
import functools

import jax
import jax.numpy as jnp
from jax import lax
from jax.experimental import pallas as pl
from jax.experimental.pallas import tpu as pltpu
from jax.sharding import PartitionSpec as P

NB = 128
TILE = 8
PANEL = 16
CHUNK = 1024
MESH = pl.DeviceIdType.MESH


def cross(left, right):
    return lax.dot_general(
        left, right, (((0,), (0,)), ((), ())), preferred_element_type=jnp.float32
    )


def dot(left, right, over=0):
    return lax.dot_general(
        left, right, (((1,), (over,)), ((), ())),
        precision=lax.Precision.HIGHEST, preferred_element_type=jnp.float32,
    )


def invert(tiles):
    count, each = len(tiles), PANEL // TILE
    shape = tiles[0].shape
    lane = lax.broadcasted_iota(jnp.int32, shape, 1)
    sub = lax.broadcasted_iota(jnp.int32, shape, 0)

    def column(t, j):
        return jnp.broadcast_to(t[:, j : j + 1], shape)

    def row(t, s):
        return jnp.broadcast_to(t[s : s + 1, :], shape)

    tiles = list(tiles)
    for base in range(0, count, each):
        start = base * TILE
        group = range(base, base + each)
        cols = [[column(tiles[i], start + k) for i in group] for k in range(PANEL)]
        inside = (lane >= start) & (lane < start + PANEL)
        held = [
            jnp.where(inside, jnp.where(lane - i * TILE == sub, 1.0, 0.0), tiles[i])
            for i in group
        ]
        for k in range(PANEL):
            at, s = divmod(k, TILE)
            on_row = sub == s
            inv = 1.0 / row(cols[k][at], s)
            c = list(cols[k])
            c[at] = jnp.where(on_row, -1.0, c[at])

            def sweep(old):
                r = row(old[at], s) * inv
                old = list(old)
                old[at] = jnp.where(on_row, 0.0, old[at])
                return [old[a] - c[a] * r for a in range(each)]

            for m in range(k + 1, PANEL):
                cols[m] = sweep(cols[m])
            held = sweep(held)
        near = range(base + each, min(base + 2 * each, count))
        far = [i for i in range(count) if i not in group and i not in near]
        for i in near:
            part = [jnp.where(inside, 0.0, tiles[i]), jnp.zeros(shape, jnp.float32)]
            for k in range(PANEL):
                at, s = divmod(k, TILE)
                part[k % 2] -= column(tiles[i], start + k) * row(held[at], s)
            tiles[i] = part[0] + part[1]
        if far:
            left = jnp.concatenate([jnp.where(inside, tiles[i], 0.0) for i in far], axis=0)
            zero = jnp.zeros(shape, jnp.float32)
            right = jnp.concatenate(
                [held[i - base] if i in group else zero for i in range(count)], axis=0
            )
            product = dot(left, right)
            for q, i in enumerate(far):
                tiles[i] = jnp.where(inside, 0.0, tiles[i]) - product[q * TILE : (q + 1) * TILE]
        for i in group:
            tiles[i] = held[i - base]
    return tiles


def eliminate(work, inverse, n, rows, first=0, hooks=()):
    def step(k, carry):
        for at, hook in hooks:
            pl.when(k == at)(hook)
        for kk in range((first or n) // NB):
            @pl.when(k == kk)
            def _():
                inverse[...] = work[kk * NB : (kk + 1) * NB, kk * NB : (kk + 1) * NB]

        tiles = invert([inverse[i : i + TILE, :] for i in range(0, NB, TILE)])
        for i, t in enumerate(tiles):
            inverse[i * TILE : (i + 1) * TILE, :] = t

        for kk in range((first or n) // NB):
            lo = kk // 2 * 2 * NB
            mid, hi = lo + NB, lo + 2 * NB
            end, limit = (first, first) if first else (n, n + rows)

            @pl.when(k == kk)
            def _():
                if kk % 2 == 0:
                    below = work[mid:hi, lo:mid]
                    scaled = dot(below, inverse[...])
                    work[mid:hi, lo:mid] = scaled
                    work[lo:mid, lo:mid] = inverse[...]
                    work[mid:hi, mid:hi] -= dot(scaled, below, 1)
                    return
                scaled = work[mid:hi, lo:mid]
                corner = dot(inverse[...], scaled)
                work[lo:mid, lo:mid] += dot(scaled.T, corner)
                work[lo:mid, mid:hi] = -corner.T
                work[mid:hi, lo:mid] = -corner
                work[mid:hi, mid:hi] = inverse[...]
                if hi == limit:
                    return
                below = work[hi:limit, lo:hi]
                ratio = dot(below, work[lo:hi, lo:hi])
                for at in range(hi, end, 2 * NB):
                    work[at:limit, at : at + 2 * NB] -= dot(
                        ratio[at - hi :], below[at - hi : at - hi + 2 * NB], 1
                    )
                work[hi:limit, lo:hi] = ratio
        return carry

    lax.fori_loop(0, (first or n) // NB, step, 0)


def finish(left, ratio, lower, rows):
    blocks, mid = len(left), lower.shape[0]
    left, ratios = list(left), []
    for b in range(blocks):
        head, below = left[b][:NB], left[b][NB:]
        inv = jnp.concatenate(
            invert([head[i : i + TILE] for i in range(0, NB, TILE)]), axis=0
        )
        if b + 1 < blocks:
            scaled = dot(below[:NB], inv)
            following = left[b + 1]
            head = following[:NB] - dot(scaled, below[:NB], 1)
            others = dot(below[NB:], inv)
            left[b + 1] = jnp.concatenate(
                [head, following[NB:] - dot(others, below[:NB], 1)], axis=0
            )
            scaled = jnp.concatenate([scaled, others], axis=0)
        else:
            scaled = dot(below, inv)
        ratios.append(scaled)
        for j in range(b + 2, blocks):
            at = (j - b - 1) * NB
            left[j] = left[j] - dot(scaled[at:], below[at : at + NB], 1)
    found = [None] * blocks
    for b in reversed(range(blocks)):
        x = ratios[b][-rows:]
        if b + 1 < blocks:
            x = x - dot(jnp.concatenate(found[b + 1 :], axis=1), ratios[b][:-rows])
        found[b] = x
    far = jnp.concatenate(found, axis=1)
    near = ratio[-rows:] - dot(far, ratio[:-rows])
    high = near[:, mid:]
    low = near[:, :mid] - dot(high, lower)
    return jnp.concatenate([low, high], axis=1), far


def substitute(work, n, rows, out_ref):
    for lo in range(n - 2 * NB, -1, -2 * NB):
        hi = lo + 2 * NB
        x = work[n : n + rows, lo:hi]
        if hi < n:
            x = x - dot(out_ref[:, hi:n], work[hi:n, lo:hi])
        out_ref[:, lo:hi] = x


def solve_kernel(cols, gram_ref, rhs_ref, out_ref, work, inverse):
    n = work.shape[1]
    rows = rhs_ref.shape[0]
    width = n // cols
    height = gram_ref.shape[1]
    for i in range(gram_ref.shape[0]):
        p, c = divmod(i, cols)
        work[p * height : (p + 1) * height, c * width : (c + 1) * width] = gram_ref[i]
    work[n : n + rows, :] = rhs_ref[...]
    eliminate(work, inverse, n, rows)
    substitute(work, n, rows, out_ref)


def solve(gram_parts, rhs, cols):
    rows, n = rhs.shape
    vmem = pl.BlockSpec(memory_space=pltpu.VMEM)
    return pl.pallas_call(
        functools.partial(solve_kernel, cols),
        out_shape=jax.ShapeDtypeStruct((rows, n), jnp.float32),
        in_specs=[vmem, vmem],
        out_specs=vmem,
        scratch_shapes=[
            pltpu.VMEM((n + rows, n), jnp.float32),
            pltpu.VMEM((NB, NB), jnp.float32),
        ],
        compiler_params=pltpu.CompilerParams(vmem_limit_bytes=48 << 20),
    )(gram_parts, rhs)


def flip(index, mask):
    total = 0
    for bit in (4, 2, 1):
        own = index // bit % 2
        total = total + bit * (1 - own if mask & bit else own)
    return total


def accumulate(total, left, right, start, count):
    total[...] = jnp.zeros_like(total)

    def chunk(i, carry):
        at = pl.ds(pl.multiple_of(start + i * CHUNK, CHUNK), CHUNK)
        total[...] += cross(left(at), right(at))
        return carry

    lax.fori_loop(0, count // CHUNK, chunk, 0)


def fused_kernel(
    point_ref, grid_ref, out_ref,
    own, sibling, received, grid, total, square_part, beside_part, project_part, cross_part,
    square_in, beside_in, project_in_x, project_in_z, cross_in, pair_sum, pair_in,
    project_sum, rhs_in,
    early, other, late, work, inverse, local_sem, send_sem, recv_sem,
):
    p, c = lax.axis_index("pair"), lax.axis_index("col")
    z, x, y, k = p // 2, p % 2, c // 2, c % 2
    count, width = own.shape
    n = work.shape[1]
    rows = out_ref.shape[0]
    mid, half = width // 2, n // 2

    barrier = pltpu.get_barrier_semaphore()
    friends = [(flip(p, d), c) for d in range(1, 8)] + [(p, flip(c, d)) for d in range(1, 4)]
    for friend in friends:
        pl.semaphore_signal(barrier, inc=1, device_id=friend, device_id_type=MESH)
    pl.semaphore_wait(barrier, len(friends))

    used = []

    def copy(at, src, dst, device):
        return pltpu.make_async_remote_copy(
            src_ref=src, dst_ref=dst, send_sem=send_sem.at[at], recv_sem=recv_sem.at[at],
            device_id=device, device_id_type=MESH,
        )

    def plan(*copies):
        base = len(used)
        used.extend(copies)
        return [functools.partial(copy, base + i, *args) for i, args in enumerate(copies)]

    def start(copies):
        for make in copies:
            make().start()

    def arrive(copies):
        for make in copies:
            make().wait_recv()

    away = pl.ds(pl.multiple_of((1 - y) * (count // 2), count // 2), count // 2)
    far = [
        plan((point_ref.at[away, pl.ds(h * mid, mid)], received.at[h], (p, flip(c, 2))))
        for h in range(2)
    ]
    beside = plan((point_ref, sibling, (p, flip(c, 1))))

    def scatter(part, landed):
        return plan(*[
            (part.at[flip(p, d)], landed.at[d - 1], (flip(p, d), c)) for d in range(1, 8)
        ])

    square_out = scatter(square_part, square_in)
    beside_out = scatter(beside_part, beside_in)
    cross_out = [scatter(cross_part.at[h], cross_in.at[h]) for h in range(2)]
    project_x = plan((project_part.at[1 - x], project_in_x, (flip(p, 1), c)))
    project_z = plan(*[
        (project_part.at[x, flip(z, d)], project_in_z.at[d - 1], (flip(z, d) * 2 + x, c))
        for d in range(1, 4)
    ])

    mine = early.at[k, x, z]
    early_z = plan(*[(mine, mine, (flip(z, d) * 2 + x, c)) for d in range(1, 4)])
    early_x = [
        plan((early.at[k, x, flip(z, d)], early.at[k, x, flip(z, d)], (flip(p, 1), c)))
        for d in range(4)
    ]
    early_core = plan((early.at[k], early.at[k], (p, flip(c, 1))))
    early_y = plan((early.at[k], other.at[k], (p, flip(c, 2))))
    other_core = plan((other.at[k], other.at[k], (p, flip(c, 1))))

    height = project_sum.shape[0] // 4

    def share(index):
        return project_sum.at[pl.ds(pl.multiple_of(index * height, height), height)]

    rhs_out = plan(*[
        (share(flip(c, d)), rhs_in.at[c], (p, flip(c, d))) for d in range(1, 4)
    ])
    depth = pair_in.shape[2]
    give = pl.ds(pl.multiple_of((1 - y) * depth, depth), depth)
    keep = pl.ds(pl.multiple_of(y * depth, depth), depth)
    pair_out = plan(
        (pair_sum.at[0, :, give], pair_in.at[0], (p, flip(c, 2))),
        (pair_sum.at[1, :, give], pair_in.at[1], (p, flip(c, 3))),
    )
    beside_x, beside_y, beside_core = (flip(p, 1), c), (p, flip(c, 2)), (p, flip(c, 1))

    def send(ref, device):
        return plan((ref, ref, device))

    late_z, late_x, late_y, late_on, late_core = [], [], [], [], []
    for block in range(2):
        piece = late.at[block, k]

        def slot(side, across, d):
            return piece.at[side, across, flip(z, d)]

        late_z.append([
            send(slot(y, x, 0), (flip(z, d) * 2 + x, c)) for d in range(1, 4)
        ])
        late_x.append([send(slot(y, x, d), beside_x) for d in range(4)])
        late_y.append([send(slot(y, x, d), beside_y) for d in range(4)])
        late_on.append([
            send(slot(1 - y, x, d), beside_x) if d % 2 else send(slot(y, 1 - x, d), beside_y)
            for d in range(4)
        ])
        late_core.append([
            send(piece.at[side, across], beside_core)
            for side, across in ((y, x), (y, 1 - x), (1 - y, x), (1 - y, 1 - x))
        ])

    def rows_of(i):
        return pl.ds(i * (count // 4), count // 4)

    def load(i, src, dst):
        return pltpu.make_async_copy(src, dst, local_sem.at[i])

    start(far[0])
    start(far[1])
    for i in range(4):
        load(i, point_ref.at[rows_of(i), :], own.at[rows_of(i), :]).start()
    start(beside)

    grid_load = load(4, grid_ref, grid)

    def deal(part, value):
        step = value.shape[0] // 8
        for q in range(8):
            part[q] = value[q * step : (q + 1) * step]

    for i in range(4):
        load(i, point_ref.at[rows_of(i), :], own.at[rows_of(i), :]).wait()
        square = cross(own[rows_of(i), :], own[rows_of(i), :])
        if i < 3:
            total[...] = square if i == 0 else total[...] + square
    square = total[...] + square
    corner = jnp.concatenate([square[: mid // 2, :mid], square[mid // 2 : mid, :mid]], axis=1)
    deal(square_part, jnp.concatenate([square[mid:], corner], axis=0))
    start(square_out)
    grid_load.start()

    arrive(beside)
    upper = total.at[pl.ds(0, mid)]

    @pl.when(k == 0)
    def _():
        accumulate(upper, lambda at: sibling[at, mid:], lambda at: own[at, :], 0, count)

    @pl.when(k == 1)
    def _():
        accumulate(upper, lambda at: own[at, :mid], lambda at: sibling[at, :], 0, count)

    deal(beside_part, upper[...])
    start(beside_out)

    grid_load.wait()
    tall = work.at[pl.ds(0, grid.shape[1]), pl.ds(0, width)]
    accumulate(tall, lambda at: grid[at, :], lambda at: own[at, :], 0, count)
    for q in range(8):
        project_part[q % 2, q // 2] = tall[q * 4 * height : (q + 1) * 4 * height, :]

    def gathered(value, landed):
        for d in range(landed.shape[0]):
            value = value + landed[d]
        return value

    cut = square_part.shape[1]
    arrive(square_out)
    mine[:cut] = gathered(square_part[p], square_in)
    arrive(beside_out)
    mine[cut:] = gathered(beside_part[p], beside_in)
    start(early_z)
    start(early_x[0])
    for d in range(1, 4):
        arrive(early_z[d - 1 : d])
        start(early_x[d])

    def cross_terms(h):
        step = mid // 8
        for block, ours in ((0, own), (1, sibling)):
            def terms(flat, product):
                def chunk(i, carry):
                    there = pl.ds(pl.multiple_of(i * CHUNK, CHUNK), CHUNK)
                    here = pl.ds(
                        pl.multiple_of(y * (count // 2) + i * CHUNK, CHUNK), CHUNK
                    )
                    flat[...] += product(received[h, there, :], ours[here, :])
                    return carry

                flat[...] = jnp.zeros_like(flat)
                lax.fori_loop(0, count // 2 // CHUNK, chunk, 0)

            @pl.when(y == 0)
            def _():
                flat = total.at[pl.ds(0, mid), :]
                terms(flat, cross)
                for q in range(8):
                    cross_part[h, q, block] = flat[q * step : (q + 1) * step, :]

            @pl.when(y == 1)
            def _():
                flat = total.at[:, pl.ds(0, mid)]
                terms(flat, lambda there, here: cross(here, there))
                for q in range(8):
                    for part in range(2):
                        at = part * mid + q * step
                        cross_part[h, q, block, :, part * mid : (part + 1) * mid] = flat[
                            at : at + step, :
                        ]

        start(cross_out[h])

    arrive(far[0])
    cross_terms(0)
    for copies in early_x:
        arrive(copies)
    start(early_core)
    start(project_x)
    arrive(early_core)

    def place(slots, at):
        def block(core, part):
            return jnp.concatenate([slots[core, q % 2, q // 2, part] for q in range(8)], axis=0)

        for core in range(2):
            lo = at + core * width
            held = block(core, slice(0, cut))
            work[lo + mid : lo + width, lo : lo + width] = held[:mid]
            work[lo : lo + mid // 2, lo : lo + mid] = held[mid:, :mid]
            work[lo + mid // 2 : lo + mid, lo : lo + mid] = held[mid:, mid:]
        lo, hi = at, at + width
        work[hi : hi + mid, lo:hi] = block(1, slice(cut, None))
        work[hi + mid : hi + width, lo:hi] = block(0, slice(cut, None))

    place(early, 0)

    def project_terms():
        arrive(project_x)
        project_part[x] += project_in_x[...]
        start(project_z)

    def rest():
        arrive(far[1])
        start(early_y)
        cross_terms(1)
        take(0)

    def take(h):
        arrive(cross_out[h])
        value = gathered(cross_part[h, p], cross_in.at[h])

        @pl.when(y == 0)
        def _():
            pair_sum[:, h] = value

        @pl.when(y == 1)
        def _():
            for part in range(2):
                pair_sum[:, part, :, h * mid : (h + 1) * mid] = value[
                    :, :, part * mid : (part + 1) * mid
                ]

    def sums():
        take(1)
        start(pair_out)
        for block in range(2):
            arrive(pair_out[block : block + 1])
            late[block, k, y, x, z] = pair_sum[block, :, keep] + pair_in[block]
            for copies in late_z[block] + [late_x[block][0], late_y[block][0]]:
                start(copies)

    def spread():
        for block in range(2):
            for d in range(1, 4):
                arrive(late_z[block][d - 1])
                start(late_x[block][d])
                start(late_y[block][d])
            start(late_core[block][0])
        arrive(early_y)
        start(other_core)
        arrive(project_z)
        project_sum[...] = gathered(project_part[x, z], project_in_z)
        start(rhs_out)
        rhs_in[c] = share(c)[...]

    def join():
        for block in range(2):
            for d in range(4):
                arrive(late_x[block][d])
                arrive(late_y[block][d])
                start(late_on[block][d])
            start(late_core[block][1])
            start(late_core[block][2])
        arrive(rhs_out)
        for col in range(4):
            @pl.when(y == 0)
            def _():
                work[n : n + rows, col * width : (col + 1) * width] = rhs_in[col]

            @pl.when(y == 1)
            def _():
                work[n : n + rows, (col ^ 2) * width : ((col ^ 2) + 1) * width] = rhs_in[col]

        arrive(other_core)
        place(other, half)
        for block in range(2):
            for d in range(4):
                arrive(late_on[block][d])
            start(late_core[block][3])
        for block in range(2):
            for copies in late_core[block]:
                arrive(copies)
        for i in range(2):
            for j in range(2):
                pieces = []
                for part in range(2):
                    for q in range(8):
                        for side in range(2):
                            core = i if i == j or side == 0 else j
                            block = 0 if i == j else 1
                            pieces.append(late[block, core, side, q % 2, q // 2, part])
                value = jnp.concatenate(pieces, axis=0)

                @pl.when(y == 0)
                def _():
                    work[half + i * width : half + (i + 1) * width, j * width : (j + 1) * width] = value

                @pl.when(y == 1)
                def _():
                    work[half + j * width : half + (j + 1) * width, i * width : (i + 1) * width] = value.T

        limit = n + rows
        low = work[half:limit, :width]
        high = work[half:limit, width:half] - dot(low, work[width:half, :width], 1)
        both = jnp.concatenate([low, high], axis=1)
        ratio = jnp.concatenate(
            [dot(low, work[:width, :width]), dot(high, work[width:half, width:half])], axis=1
        )
        head = work[half : half + NB, half : half + NB] - dot(ratio[:NB], both[:NB], 1)
        panel = work[half + NB : limit, half : half + width] - dot(ratio[NB:], both[:width], 1)
        last = work[half + width : limit, half + width : n] - dot(
            ratio[width:], both[width:half], 1
        )
        left = [
            jnp.concatenate([head, panel[:, :NB]], axis=0),
            panel[:, NB:],
            last[:, :NB],
            last[NB:, NB:],
        ]
        return finish(left, ratio, work[width:half, :width], rows)

    hooks = ((0, rest), (1, project_terms), (2, sums), (3, spread))
    eliminate(work, inverse, n, rows, half, hooks)
    near, far_side = join()

    @pl.when(y == 0)
    def _():
        out_ref[:, :half] = near
        out_ref[:, half:] = far_side

    @pl.when(y == 1)
    def _():
        out_ref[:, :half] = far_side
        out_ref[:, half:] = near

    for i, args in enumerate(used):
        copy(i, *args).wait_send()


def fused(point_values, grid_values):
    count, width = point_values.shape
    rows_all = grid_values.shape[1]
    n = 4 * width
    rows = rows_all // 32
    cut, side, deep = width * 3 // 32, width // 16, width // 16
    f32, bf16 = jnp.float32, jnp.bfloat16

    def buffer(*shape, dtype=f32):
        return pltpu.VMEM(shape, dtype)

    hbm = pl.BlockSpec(memory_space=pl.ANY)
    return pl.pallas_call(
        fused_kernel,
        out_shape=jax.ShapeDtypeStruct((rows, n), f32),
        in_specs=[hbm, hbm],
        out_specs=pl.BlockSpec(memory_space=pltpu.VMEM),
        scratch_shapes=[
            buffer(count, width, dtype=bf16),
            buffer(count, width, dtype=bf16),
            buffer(2, count // 2, width // 2, dtype=bf16),
            buffer(count, rows_all, dtype=bf16),
            buffer(width, width),
            buffer(8, cut, width),
            buffer(8, side, width),
            buffer(2, 4, rows_all // 8, width),
            buffer(2, 8, 2, deep, width),
            buffer(7, cut, width),
            buffer(7, side, width),
            buffer(4, rows_all // 8, width),
            buffer(3, rows_all // 8, width),
            buffer(2, 7, 2, deep, width),
            buffer(2, 2, deep, width),
            buffer(2, 2, deep // 2, width),
            buffer(rows_all // 8, width),
            buffer(4, rows, width),
            buffer(2, 2, 4, cut + side, width),
            buffer(2, 2, 4, cut + side, width),
            buffer(2, 2, 2, 2, 4, 2, deep // 2, width),
            buffer(n + rows, n),
            buffer(NB, NB),
            pltpu.SemaphoreType.DMA((5,)),
            pltpu.SemaphoreType.DMA((112,)),
            pltpu.SemaphoreType.DMA((112,)),
        ],
        compiler_params=pltpu.CompilerParams(
            collective_id=0, has_side_effects=True, vmem_limit_bytes=52 << 20
        ),
    )(point_values, grid_values)


def solution(mesh):
    cols, pairs = mesh.shape["col"], mesh.shape["pair"]

    def body(point_values, grid_values):
        if cols == 4 and pairs == 8:
            return fused(point_values, grid_values)
        project = cross(grid_values, point_values)
        gathered = lax.all_gather(point_values, "col", axis=1, tiled=True)
        gram = cross(gathered, point_values)
        width = gram.shape[1]
        both = jnp.concatenate(
            [gram.reshape(pairs, -1, width), project.reshape(pairs, -1, width)], axis=1
        )
        exchanged = lax.all_to_all(both, "pair", split_axis=0, concat_axis=0, tiled=True)
        own = jnp.sum(exchanged, axis=0)
        height = gram.shape[0] // pairs
        gram_parts = lax.all_gather(own[:height], ("pair", "col"), axis=0, tiled=False)
        regrouped = lax.all_to_all(own[height:], "col", split_axis=0, concat_axis=1, tiled=True)
        return solve(gram_parts, regrouped, cols)

    in_specs = (P("pair", "col"), P("pair", None))
    out_specs = P(("pair", "col"), None)
    return jax.shard_map(body, mesh=mesh, in_specs=in_specs, out_specs=out_specs, check_vma=False)
```

```python
import functools

import jax
import jax.numpy as jnp
from jax import lax
from jax.experimental import pallas as pl
from jax.experimental.pallas import tpu as pltpu
from jax.sharding import PartitionSpec as P

NB = 128
TILE = 8
PANEL = 16
CHUNK = 1024
MESH = pl.DeviceIdType.MESH


def cross(left, right):
    return lax.dot_general(
        left, right, (((0,), (0,)), ((), ())), preferred_element_type=jnp.float32
    )


def dot(left, right, over=0):
    return lax.dot_general(
        left, right, (((1,), (over,)), ((), ())),
        precision=lax.Precision.HIGHEST, preferred_element_type=jnp.float32,
    )


def invert(tiles):
    count, each = len(tiles), PANEL // TILE
    shape = tiles[0].shape
    lane = lax.broadcasted_iota(jnp.int32, shape, 1)
    sub = lax.broadcasted_iota(jnp.int32, shape, 0)

    def column(t, j):
        return jnp.broadcast_to(t[:, j : j + 1], shape)

    def row(t, s):
        return jnp.broadcast_to(t[s : s + 1, :], shape)

    tiles = list(tiles)
    for base in range(0, count, each):
        start = base * TILE
        group = range(base, base + each)
        cols = [[column(tiles[i], start + k) for i in group] for k in range(PANEL)]
        inside = (lane >= start) & (lane < start + PANEL)
        held = [
            jnp.where(inside, jnp.where(lane - i * TILE == sub, 1.0, 0.0), tiles[i])
            for i in group
        ]
        for k in range(PANEL):
            at, s = divmod(k, TILE)
            on_row = sub == s
            inv = 1.0 / row(cols[k][at], s)
            c = list(cols[k])
            c[at] = jnp.where(on_row, -1.0, c[at])

            def sweep(old):
                r = row(old[at], s) * inv
                old = list(old)
                old[at] = jnp.where(on_row, 0.0, old[at])
                return [old[a] - c[a] * r for a in range(each)]

            for m in range(k + 1, PANEL):
                cols[m] = sweep(cols[m])
            held = sweep(held)
        near = range(base + each, min(base + 2 * each, count))
        far = [i for i in range(count) if i not in group and i not in near]
        for i in near:
            part = [jnp.where(inside, 0.0, tiles[i]), jnp.zeros(shape, jnp.float32)]
            for k in range(PANEL):
                at, s = divmod(k, TILE)
                part[k % 2] -= column(tiles[i], start + k) * row(held[at], s)
            tiles[i] = part[0] + part[1]
        if far:
            left = jnp.concatenate([jnp.where(inside, tiles[i], 0.0) for i in far], axis=0)
            zero = jnp.zeros(shape, jnp.float32)
            right = jnp.concatenate(
                [held[i - base] if i in group else zero for i in range(count)], axis=0
            )
            product = dot(left, right)
            for q, i in enumerate(far):
                tiles[i] = jnp.where(inside, 0.0, tiles[i]) - product[q * TILE : (q + 1) * TILE]
        for i in group:
            tiles[i] = held[i - base]
    return tiles


def eliminate(work, inverse, n, rows, first=0, hooks=()):
    def step(k, carry):
        for at, hook in hooks:
            pl.when(k == at)(hook)
        for kk in range((first or n) // NB):
            @pl.when(k == kk)
            def _():
                inverse[...] = work[kk * NB : (kk + 1) * NB, kk * NB : (kk + 1) * NB]

        tiles = invert([inverse[i : i + TILE, :] for i in range(0, NB, TILE)])
        for i, t in enumerate(tiles):
            inverse[i * TILE : (i + 1) * TILE, :] = t

        for kk in range((first or n) // NB):
            lo = kk // 2 * 2 * NB
            mid, hi = lo + NB, lo + 2 * NB
            end, limit = (first, first) if first else (n, n + rows)

            @pl.when(k == kk)
            def _():
                if kk % 2 == 0:
                    below = work[mid:hi, lo:mid]
                    scaled = dot(below, inverse[...])
                    work[mid:hi, lo:mid] = scaled
                    work[lo:mid, lo:mid] = inverse[...]
                    work[mid:hi, mid:hi] -= dot(scaled, below, 1)
                    return
                scaled = work[mid:hi, lo:mid]
                corner = dot(inverse[...], scaled)
                work[lo:mid, lo:mid] += dot(scaled.T, corner)
                work[lo:mid, mid:hi] = -corner.T
                work[mid:hi, lo:mid] = -corner
                work[mid:hi, mid:hi] = inverse[...]
                if hi == limit:
                    return
                below = work[hi:limit, lo:hi]
                ratio = dot(below, work[lo:hi, lo:hi])
                for at in range(hi, end, 2 * NB):
                    work[at:limit, at : at + 2 * NB] -= dot(
                        ratio[at - hi :], below[at - hi : at - hi + 2 * NB], 1
                    )
                work[hi:limit, lo:hi] = ratio
        return carry

    lax.fori_loop(0, (first or n) // NB, step, 0)


def finish(left, ratio, lower, rows):
    blocks, mid = len(left), lower.shape[0]
    left, ratios = list(left), []
    for b in range(blocks):
        head, below = left[b][:NB], left[b][NB:]
        inv = jnp.concatenate(
            invert([head[i : i + TILE] for i in range(0, NB, TILE)]), axis=0
        )
        if b + 1 < blocks:
            scaled = dot(below[:NB], inv)
            following = left[b + 1]
            head = following[:NB] - dot(scaled, below[:NB], 1)
            others = dot(below[NB:], inv)
            left[b + 1] = jnp.concatenate(
                [head, following[NB:] - dot(others, below[:NB], 1)], axis=0
            )
            scaled = jnp.concatenate([scaled, others], axis=0)
        else:
            scaled = dot(below, inv)
        ratios.append(scaled)
        for j in range(b + 2, blocks):
            at = (j - b - 1) * NB
            left[j] = left[j] - dot(scaled[at:], below[at : at + NB], 1)
    found = [None] * blocks
    for b in reversed(range(blocks)):
        x = ratios[b][-rows:]
        if b + 1 < blocks:
            x = x - dot(jnp.concatenate(found[b + 1 :], axis=1), ratios[b][:-rows])
        found[b] = x
    far = jnp.concatenate(found, axis=1)
    near = ratio[-rows:] - dot(far, ratio[:-rows])
    high = near[:, mid:]
    low = near[:, :mid] - dot(high, lower)
    return jnp.concatenate([low, high], axis=1), far


def substitute(work, n, rows, out_ref):
    for lo in range(n - 2 * NB, -1, -2 * NB):
        hi = lo + 2 * NB
        x = work[n : n + rows, lo:hi]
        if hi < n:
            x = x - dot(out_ref[:, hi:n], work[hi:n, lo:hi])
        out_ref[:, lo:hi] = x


def solve_kernel(cols, gram_ref, rhs_ref, out_ref, work, inverse):
    n = work.shape[1]
    rows = rhs_ref.shape[0]
    width = n // cols
    height = gram_ref.shape[1]
    for i in range(gram_ref.shape[0]):
        p, c = divmod(i, cols)
        work[p * height : (p + 1) * height, c * width : (c + 1) * width] = gram_ref[i]
    work[n : n + rows, :] = rhs_ref[...]
    eliminate(work, inverse, n, rows)
    substitute(work, n, rows, out_ref)


def solve(gram_parts, rhs, cols):
    rows, n = rhs.shape
    vmem = pl.BlockSpec(memory_space=pltpu.VMEM)
    return pl.pallas_call(
        functools.partial(solve_kernel, cols),
        out_shape=jax.ShapeDtypeStruct((rows, n), jnp.float32),
        in_specs=[vmem, vmem],
        out_specs=vmem,
        scratch_shapes=[
            pltpu.VMEM((n + rows, n), jnp.float32),
            pltpu.VMEM((NB, NB), jnp.float32),
        ],
        compiler_params=pltpu.CompilerParams(vmem_limit_bytes=48 << 20),
    )(gram_parts, rhs)


def flip(index, mask):
    total = 0
    for bit in (4, 2, 1):
        own = index // bit % 2
        total = total + bit * (1 - own if mask & bit else own)
    return total


def accumulate(total, left, right, start, count):
    total[...] = jnp.zeros_like(total)

    def chunk(i, carry):
        at = pl.ds(pl.multiple_of(start + i * CHUNK, CHUNK), CHUNK)
        total[...] += cross(left(at), right(at))
        return carry

    lax.fori_loop(0, count // CHUNK, chunk, 0)


def fused_kernel(
    point_ref, grid_ref, out_ref,
    own, sibling, received, grid, total, square_part, beside_part, project_part, cross_part,
    square_in, beside_in, project_in_x, project_in_z, cross_in, pair_sum, pair_in,
    project_sum, rhs_in,
    early, other, late, work, inverse, local_sem, send_sem, recv_sem,
):
    p, c = lax.axis_index("pair"), lax.axis_index("col")
    z, x, y, k = p // 2, p % 2, c // 2, c % 2
    count, width = own.shape
    n = work.shape[1]
    rows = out_ref.shape[0]
    mid, half = width // 2, n // 2

    barrier = pltpu.get_barrier_semaphore()
    friends = [(flip(p, d), c) for d in range(1, 8)] + [(p, flip(c, d)) for d in range(1, 4)]
    for friend in friends:
        pl.semaphore_signal(barrier, inc=1, device_id=friend, device_id_type=MESH)
    pl.semaphore_wait(barrier, len(friends))

    used = []

    def copy(at, src, dst, device):
        return pltpu.make_async_remote_copy(
            src_ref=src, dst_ref=dst, send_sem=send_sem.at[at], recv_sem=recv_sem.at[at],
            device_id=device, device_id_type=MESH,
        )

    def plan(*copies):
        base = len(used)
        used.extend(copies)
        return [functools.partial(copy, base + i, *args) for i, args in enumerate(copies)]

    def start(copies):
        for make in copies:
            make().start()

    def arrive(copies):
        for make in copies:
            make().wait_recv()

    away = pl.ds(pl.multiple_of((1 - y) * (count // 2), count // 2), count // 2)
    far = [
        plan((point_ref.at[away, pl.ds(h * mid, mid)], received.at[h], (p, flip(c, 2))))
        for h in range(2)
    ]
    beside = plan((point_ref, sibling, (p, flip(c, 1))))

    def scatter(part, landed):
        return plan(*[
            (part.at[flip(p, d)], landed.at[d - 1], (flip(p, d), c)) for d in range(1, 8)
        ])

    square_out = scatter(square_part, square_in)
    beside_out = scatter(beside_part, beside_in)
    cross_out = [scatter(cross_part.at[h], cross_in.at[h]) for h in range(2)]
    project_x = plan((project_part.at[1 - x], project_in_x, (flip(p, 1), c)))
    project_z = plan(*[
        (project_part.at[x, flip(z, d)], project_in_z.at[d - 1], (flip(z, d) * 2 + x, c))
        for d in range(1, 4)
    ])

    mine = early.at[k, x, z]
    early_z = plan(*[(mine, mine, (flip(z, d) * 2 + x, c)) for d in range(1, 4)])
    early_x = [
        plan((early.at[k, x, flip(z, d)], early.at[k, x, flip(z, d)], (flip(p, 1), c)))
        for d in range(4)
    ]
    early_core = plan((early.at[k], early.at[k], (p, flip(c, 1))))
    early_y = plan((early.at[k], other.at[k], (p, flip(c, 2))))
    other_core = plan((other.at[k], other.at[k], (p, flip(c, 1))))

    height = project_sum.shape[0] // 4

    def share(index):
        return project_sum.at[pl.ds(pl.multiple_of(index * height, height), height)]

    rhs_out = plan(*[
        (share(flip(c, d)), rhs_in.at[c], (p, flip(c, d))) for d in range(1, 4)
    ])
    depth = pair_in.shape[2]
    give = pl.ds(pl.multiple_of((1 - y) * depth, depth), depth)
    keep = pl.ds(pl.multiple_of(y * depth, depth), depth)
    pair_out = plan(
        (pair_sum.at[0, :, give], pair_in.at[0], (p, flip(c, 2))),
        (pair_sum.at[1, :, give], pair_in.at[1], (p, flip(c, 3))),
    )
    beside_x, beside_y, beside_core = (flip(p, 1), c), (p, flip(c, 2)), (p, flip(c, 1))

    def send(ref, device):
        return plan((ref, ref, device))

    late_z, late_x, late_y, late_on, late_core = [], [], [], [], []
    for block in range(2):
        piece = late.at[block, k]

        def slot(side, across, d):
            return piece.at[side, across, flip(z, d)]

        late_z.append([
            send(slot(y, x, 0), (flip(z, d) * 2 + x, c)) for d in range(1, 4)
        ])
        late_x.append([send(slot(y, x, d), beside_x) for d in range(4)])
        late_y.append([send(slot(y, x, d), beside_y) for d in range(4)])
        late_on.append([
            send(slot(1 - y, x, d), beside_x) if d % 2 else send(slot(y, 1 - x, d), beside_y)
            for d in range(4)
        ])
        late_core.append([
            send(piece.at[side, across], beside_core)
            for side, across in ((y, x), (y, 1 - x), (1 - y, x), (1 - y, 1 - x))
        ])

    def rows_of(i):
        return pl.ds(i * (count // 4), count // 4)

    def load(i, src, dst):
        return pltpu.make_async_copy(src, dst, local_sem.at[i])

    start(far[0])
    start(far[1])
    for i in range(4):
        load(i, point_ref.at[rows_of(i), :], own.at[rows_of(i), :]).start()
    start(beside)

    grid_load = load(4, grid_ref, grid)

    def deal(part, value):
        step = value.shape[0] // 8
        for q in range(8):
            part[q] = value[q * step : (q + 1) * step]

    for i in range(4):
        load(i, point_ref.at[rows_of(i), :], own.at[rows_of(i), :]).wait()
        square = cross(own[rows_of(i), :], own[rows_of(i), :])
        if i < 3:
            total[...] = square if i == 0 else total[...] + square
    square = total[...] + square
    corner = jnp.concatenate([square[: mid // 2, :mid], square[mid // 2 : mid, :mid]], axis=1)
    deal(square_part, jnp.concatenate([square[mid:], corner], axis=0))
    start(square_out)
    grid_load.start()

    arrive(beside)
    upper = total.at[pl.ds(0, mid)]

    @pl.when(k == 0)
    def _():
        accumulate(upper, lambda at: sibling[at, mid:], lambda at: own[at, :], 0, count)

    @pl.when(k == 1)
    def _():
        accumulate(upper, lambda at: own[at, :mid], lambda at: sibling[at, :], 0, count)

    deal(beside_part, upper[...])
    start(beside_out)

    grid_load.wait()
    tall = work.at[pl.ds(0, grid.shape[1]), pl.ds(0, width)]
    accumulate(tall, lambda at: grid[at, :], lambda at: own[at, :], 0, count)
    for q in range(8):
        project_part[q % 2, q // 2] = tall[q * 4 * height : (q + 1) * 4 * height, :]

    def gathered(value, landed):
        for d in range(landed.shape[0]):
            value = value + landed[d]
        return value

    cut = square_part.shape[1]
    arrive(square_out)
    mine[:cut] = gathered(square_part[p], square_in)
    arrive(beside_out)
    mine[cut:] = gathered(beside_part[p], beside_in)
    start(early_z)
    start(early_x[0])
    for d in range(1, 4):
        arrive(early_z[d - 1 : d])
        start(early_x[d])

    def cross_terms(h):
        step = mid // 8
        for block, ours in ((0, own), (1, sibling)):
            def terms(flat, product):
                def chunk(i, carry):
                    there = pl.ds(pl.multiple_of(i * CHUNK, CHUNK), CHUNK)
                    here = pl.ds(
                        pl.multiple_of(y * (count // 2) + i * CHUNK, CHUNK), CHUNK
                    )
                    flat[...] += product(received[h, there, :], ours[here, :])
                    return carry

                flat[...] = jnp.zeros_like(flat)
                lax.fori_loop(0, count // 2 // CHUNK, chunk, 0)

            @pl.when(y == 0)
            def _():
                flat = total.at[pl.ds(0, mid), :]
                terms(flat, cross)
                for q in range(8):
                    cross_part[h, q, block] = flat[q * step : (q + 1) * step, :]

            @pl.when(y == 1)
            def _():
                flat = total.at[:, pl.ds(0, mid)]
                terms(flat, lambda there, here: cross(here, there))
                for q in range(8):
                    for part in range(2):
                        at = part * mid + q * step
                        cross_part[h, q, block, :, part * mid : (part + 1) * mid] = flat[
                            at : at + step, :
                        ]

        start(cross_out[h])

    arrive(far[0])
    cross_terms(0)
    for copies in early_x:
        arrive(copies)
    start(early_core)
    start(project_x)
    arrive(early_core)

    def place(slots, at):
        def block(core, part):
            return jnp.concatenate([slots[core, q % 2, q // 2, part] for q in range(8)], axis=0)

        for core in range(2):
            lo = at + core * width
            held = block(core, slice(0, cut))
            work[lo + mid : lo + width, lo : lo + width] = held[:mid]
            work[lo : lo + mid // 2, lo : lo + mid] = held[mid:, :mid]
            work[lo + mid // 2 : lo + mid, lo : lo + mid] = held[mid:, mid:]
        lo, hi = at, at + width
        work[hi : hi + mid, lo:hi] = block(1, slice(cut, None))
        work[hi + mid : hi + width, lo:hi] = block(0, slice(cut, None))

    place(early, 0)

    def project_terms():
        arrive(project_x)
        project_part[x] += project_in_x[...]

    def rest():
        arrive(far[1])
        start(early_y)
        cross_terms(1)
        take(0)

    def take(h):
        arrive(cross_out[h])
        value = gathered(cross_part[h, p], cross_in.at[h])

        @pl.when(y == 0)
        def _():
            pair_sum[:, h] = value

        @pl.when(y == 1)
        def _():
            for part in range(2):
                pair_sum[:, part, :, h * mid : (h + 1) * mid] = value[
                    :, :, part * mid : (part + 1) * mid
                ]

    def sums():
        take(1)
        start(pair_out)
        for block in range(2):
            arrive(pair_out[block : block + 1])
            late[block, k, y, x, z] = pair_sum[block, :, keep] + pair_in[block]
            for copies in late_z[block] + [late_x[block][0], late_y[block][0]]:
                start(copies)

    def spread():
        for block in range(2):
            for d in range(1, 4):
                arrive(late_z[block][d - 1])
                start(late_x[block][d])
                start(late_y[block][d])
            start(late_core[block][0])
        start(project_z)
        arrive(early_y)
        start(other_core)

    def join():
        for block in range(2):
            for d in range(4):
                arrive(late_x[block][d])
                arrive(late_y[block][d])
                start(late_on[block][d])
            start(late_core[block][1])
            start(late_core[block][2])
        arrive(project_z)
        project_sum[...] = gathered(project_part[x, z], project_in_z)
        start(rhs_out)
        rhs_in[c] = share(c)[...]
        arrive(other_core)
        place(other, half)
        for block in range(2):
            for d in range(4):
                arrive(late_on[block][d])
            start(late_core[block][3])
        arrive(rhs_out)
        for col in range(4):
            @pl.when(y == 0)
            def _():
                work[n : n + rows, col * width : (col + 1) * width] = rhs_in[col]

            @pl.when(y == 1)
            def _():
                work[n : n + rows, (col ^ 2) * width : ((col ^ 2) + 1) * width] = rhs_in[col]

        for block in range(2):
            for copies in late_core[block]:
                arrive(copies)
        for i in range(2):
            for j in range(2):
                pieces = []
                for part in range(2):
                    for q in range(8):
                        for side in range(2):
                            core = i if i == j or side == 0 else j
                            block = 0 if i == j else 1
                            pieces.append(late[block, core, side, q % 2, q // 2, part])
                value = jnp.concatenate(pieces, axis=0)

                @pl.when(y == 0)
                def _():
                    work[half + i * width : half + (i + 1) * width, j * width : (j + 1) * width] = value

                @pl.when(y == 1)
                def _():
                    work[half + j * width : half + (j + 1) * width, i * width : (i + 1) * width] = value.T

        limit = n + rows
        low = work[half:limit, :width]
        high = work[half:limit, width:half] - dot(low, work[width:half, :width], 1)
        both = jnp.concatenate([low, high], axis=1)
        ratio = jnp.concatenate(
            [dot(low, work[:width, :width]), dot(high, work[width:half, width:half])], axis=1
        )
        head = work[half : half + NB, half : half + NB] - dot(ratio[:NB], both[:NB], 1)
        panel = work[half + NB : limit, half : half + width] - dot(ratio[NB:], both[:width], 1)
        last = work[half + width : limit, half + width : n] - dot(
            ratio[width:], both[width:half], 1
        )
        left = [
            jnp.concatenate([head, panel[:, :NB]], axis=0),
            panel[:, NB:],
            last[:, :NB],
            last[NB:, NB:],
        ]
        return finish(left, ratio, work[width:half, :width], rows)

    hooks = ((0, rest), (1, project_terms), (2, sums), (3, spread))
    eliminate(work, inverse, n, rows, half, hooks)
    near, far_side = join()

    @pl.when(y == 0)
    def _():
        out_ref[:, :half] = near
        out_ref[:, half:] = far_side

    @pl.when(y == 1)
    def _():
        out_ref[:, :half] = far_side
        out_ref[:, half:] = near

    for i, args in enumerate(used):
        copy(i, *args).wait_send()


def fused(point_values, grid_values):
    count, width = point_values.shape
    rows_all = grid_values.shape[1]
    n = 4 * width
    rows = rows_all // 32
    cut, side, deep = width * 3 // 32, width // 16, width // 16
    f32, bf16 = jnp.float32, jnp.bfloat16

    def buffer(*shape, dtype=f32):
        return pltpu.VMEM(shape, dtype)

    hbm = pl.BlockSpec(memory_space=pl.ANY)
    return pl.pallas_call(
        fused_kernel,
        out_shape=jax.ShapeDtypeStruct((rows, n), f32),
        in_specs=[hbm, hbm],
        out_specs=pl.BlockSpec(memory_space=pltpu.VMEM),
        scratch_shapes=[
            buffer(count, width, dtype=bf16),
            buffer(count, width, dtype=bf16),
            buffer(2, count // 2, width // 2, dtype=bf16),
            buffer(count, rows_all, dtype=bf16),
            buffer(width, width),
            buffer(8, cut, width),
            buffer(8, side, width),
            buffer(2, 4, rows_all // 8, width),
            buffer(2, 8, 2, deep, width),
            buffer(7, cut, width),
            buffer(7, side, width),
            buffer(4, rows_all // 8, width),
            buffer(3, rows_all // 8, width),
            buffer(2, 7, 2, deep, width),
            buffer(2, 2, deep, width),
            buffer(2, 2, deep // 2, width),
            buffer(rows_all // 8, width),
            buffer(4, rows, width),
            buffer(2, 2, 4, cut + side, width),
            buffer(2, 2, 4, cut + side, width),
            buffer(2, 2, 2, 2, 4, 2, deep // 2, width),
            buffer(n + rows, n),
            buffer(NB, NB),
            pltpu.SemaphoreType.DMA((5,)),
            pltpu.SemaphoreType.DMA((112,)),
            pltpu.SemaphoreType.DMA((112,)),
        ],
        compiler_params=pltpu.CompilerParams(
            collective_id=0, has_side_effects=True, vmem_limit_bytes=52 << 20
        ),
    )(point_values, grid_values)


def solution(mesh):
    cols, pairs = mesh.shape["col"], mesh.shape["pair"]

    def body(point_values, grid_values):
        if cols == 4 and pairs == 8:
            return fused(point_values, grid_values)
        project = cross(grid_values, point_values)
        gathered = lax.all_gather(point_values, "col", axis=1, tiled=True)
        gram = cross(gathered, point_values)
        width = gram.shape[1]
        both = jnp.concatenate(
            [gram.reshape(pairs, -1, width), project.reshape(pairs, -1, width)], axis=1
        )
        exchanged = lax.all_to_all(both, "pair", split_axis=0, concat_axis=0, tiled=True)
        own = jnp.sum(exchanged, axis=0)
        height = gram.shape[0] // pairs
        gram_parts = lax.all_gather(own[:height], ("pair", "col"), axis=0, tiled=False)
        regrouped = lax.all_to_all(own[height:], "col", split_axis=0, concat_axis=1, tiled=True)
        return solve(gram_parts, regrouped, cols)

    in_specs = (P("pair", "col"), P("pair", None))
    out_specs = P(("pair", "col"), None)
    return jax.shard_map(body, mesh=mesh, in_specs=in_specs, out_specs=out_specs, check_vma=False)
```
